32 devices in a mesh: table: 4 (over y, core), cand: 8 (over z, x).
Axes of the slice: x: 2, y: 2, z: 4, core: 2. Of those that a mesh axis runs over, the one named last changes fastest.
Arguments:
- user_feats: bfloat16 [16, 4096], P('cand'), may hold values from -6 to 6
- tower_weight: bfloat16 [4096, 4096], P(None, 'table'), may hold values from -0.09375 to 0.09375
- tower_bias: float32 [4096], P('table'), may hold values from -3 to 3
- user_proj: bfloat16 [4096, 1024], P('table'), may hold values from -0.09375 to 0.09375
- item_ids: int32 [8, 16, 512], P('table', None, 'cand'), may hold values from 0 to 65535, as said below
- tables: bfloat16 [8, 65536, 128], P('table', 'cand'), may hold values from -6 to 6
- cross_weight: bfloat16 [1024, 1024], replicated, may hold values from -0.1875 to 0.1875
- cross_bias: float32 [1024], replicated, may hold values from -1 to 1
- mlp_first: bfloat16 [1024, 4096], P(None, 'table'), may hold values from -0.1875 to 0.1875
- first_bias: float32 [4096], P('table'), may hold values from -3 to 3
- mlp_second: bfloat16 [4096, 1024], P('table'), may hold values from -0.09375 to 0.09375
- second_bias: float32 [1024], replicated, may hold values from -3 to 3
- task_weight: bfloat16 [1024, 8], replicated, may hold values from -0.1875 to 0.1875
- task_bias: float32 [8], replicated, may hold values from -4 to 4
Outputs:
- logits: float32 [8, 16, 512], P(None, 'table', 'cand')
The draws below stay inside these ranges and needn't reach their ends.
Inputs may be any that keep to these rules, and one draw needn't show every extreme that they name: `item_ids`: rows k * 8192 to (k + 1) * 8192 - 1 of a table lie on index k of cand. For each table and each index of cand, that device's candidates of all requests name at most 256 ids lying on any one index of cand, and exactly 256 for one of them.
All inputs are finite; a program needn't handle non-finite values.
Results may differ from the reference program's by a relative error of at most 0.014.
Values may be sent and summed in bfloat16 or wider, within the bound.
A program may use at most 128 MiB of HBM per device.

```python
import jax
import jax.numpy as jnp
from jax import lax

DU = 4096
E = 128
HID = 4096
TOP = 1024
TASKS = 8
ROWS_DEV = 8192
CAND_DEV = 64
REQUESTS = 16
CANDS = 512
NTAB = 8
VOCAB = 65536
D0 = 1024
CAP = 256
N_CAND = 8


def draw_item_ids(key, part):
    row_count = REQUESTS * CAND_DEV
    key_hot, key_rows, key_perm = jax.random.split(jax.random.fold_in(key, 11), 3)
    hottest = jax.random.randint(key_hot, (NTAB, N_CAND), 0, N_CAND)
    hottest = hottest.at[0, 0].set(N_CAND - 1)
    places = jnp.arange(row_count)[None, None, :]
    spread = (places - CAP) % (N_CAND - 1)
    spread = spread + (spread >= hottest[:, :, None]).astype(jnp.int32)
    owners = jnp.where(places < CAP, hottest[:, :, None], spread)
    local_rows = jax.random.randint(key_rows, (NTAB, N_CAND, row_count), 0, ROWS_DEV)
    local_rows = jnp.where(places == 0, ROWS_DEV - 1, local_rows)
    joined = (owners * ROWS_DEV + local_rows).reshape(NTAB * N_CAND, row_count)
    perm_keys = jax.random.split(key_perm, NTAB * N_CAND)

    def shuffle(one_key, values):
        return jax.random.permutation(one_key, values)
    mixed = jax.vmap(shuffle)(perm_keys, joined)
    mixed = mixed.reshape(NTAB, N_CAND, REQUESTS, CAND_DEV)
    mixed = jnp.transpose(mixed, (0, 2, 1, 3)).reshape(NTAB, REQUESTS, CANDS)
    return mixed.astype(jnp.int32)


def block_levels(rng, shape, pieces, least, top_value):
    def one(position, shards_of):
        draws = jax.random.uniform(jax.random.fold_in(jax.random.fold_in(rng, 6), position), (shards_of,), jnp.float32, least / len(pieces), top_value / len(pieces))
        return jnp.repeat(jnp.exp(draws), shape[position] // shards_of).reshape((-1,) + (1,) * (len(shape) - position - 1))

    factor_of = one(*pieces[0])
    for cut in pieces[1:]:
        factor_of = factor_of * one(*cut)
    return factor_of


def bell_draw(own_key, extent, scale, bound, cuts=(), held_as=jnp.bfloat16):
    values = scale * jax.random.normal(own_key, extent, jnp.float32)
    if cuts:
        values = values * block_levels(own_key, extent, cuts, -0.22, 0.18)
    return jnp.clip(values, -bound, bound).astype(held_as)


def setup_inputs(seed: int = 0) -> dict:
    streams_of = jax.random.split(jax.random.key(seed), 15)
    return {
        "user_feats": bell_draw(streams_of[0], (REQUESTS, DU), 1.0, 6.0, ((0, 8),)),
        "tower_weight": bell_draw(streams_of[1], (DU, DU), DU ** -0.5, 0.09375, ((1, 4),)),
        "tower_bias": bell_draw(streams_of[2], (DU,), 0.5, 3.0, ((0, 4),), jnp.float32),
        "user_proj": bell_draw(streams_of[3], (DU, D0), DU ** -0.5, 0.09375, ((0, 4),)),
        "item_ids": draw_item_ids(jax.random.fold_in(streams_of[14], 71), 0),
        "tables": bell_draw(streams_of[5], (NTAB, VOCAB, E), 1.0, 6.0, ((0, 4), (1, 8))),
        "cross_weight": bell_draw(streams_of[6], (D0, D0), D0 ** -0.5, 0.1875),
        "cross_bias": jnp.clip(jax.random.uniform(streams_of[7], (D0,), jnp.float32, -1.0, 1.0), -1.0, 1.0),
        "mlp_first": bell_draw(streams_of[8], (D0, HID), D0 ** -0.5, 0.1875, ((1, 4),)),
        "first_bias": bell_draw(streams_of[9], (HID,), 0.5, 3.0, ((0, 4),), jnp.float32),
        "mlp_second": bell_draw(streams_of[10], (HID, TOP), HID ** -0.5, 0.09375, ((0, 4),)),
        "second_bias": bell_draw(streams_of[11], (TOP,), 0.5, 3.0, (), jnp.float32),
        "task_weight": bell_draw(streams_of[12], (TOP, TASKS), TOP ** -0.5, 0.1875),
        "task_bias": bell_draw(streams_of[13], (TASKS,), 1.0, 4.0, (), jnp.float32),
    }


def reference(user_feats, tower_weight, tower_bias, user_proj, item_ids, tables, cross_weight, cross_bias, mlp_first, first_bias, mlp_second, second_bias, task_weight, task_bias):
    tower = jax.nn.relu(jnp.dot(user_feats, tower_weight, preferred_element_type=jnp.float32) + tower_bias).astype(jnp.bfloat16)
    projected = jnp.dot(tower, user_proj, preferred_element_type=jnp.float32).astype(jnp.bfloat16)

    def pick_rows(table_rows, wanted):
        return jnp.take(table_rows, wanted, axis=0)

    def one_request(packed):
        request_ids, request_proj = packed
        fetched = jax.vmap(pick_rows)(tables, request_ids)
        joined = jnp.transpose(fetched, (1, 0, 2)).reshape(CANDS, NTAB * E)
        base = (joined.astype(jnp.float32) + request_proj.astype(jnp.float32)[None, :]).astype(jnp.bfloat16)
        product = jnp.dot(base, cross_weight, preferred_element_type=jnp.float32)
        base_wide = base.astype(jnp.float32)
        crossed = (base_wide * (product + cross_bias) + base_wide).astype(jnp.bfloat16)
        hidden = jax.nn.relu(jnp.dot(crossed, mlp_first, preferred_element_type=jnp.float32) + first_bias).astype(jnp.bfloat16)
        top = jax.nn.relu(jnp.dot(hidden, mlp_second, preferred_element_type=jnp.float32) + second_bias).astype(jnp.bfloat16)
        scores = jnp.dot(top, task_weight, preferred_element_type=jnp.float32) + task_bias
        return jnp.transpose(scores, (1, 0))

    result = lax.map(one_request, (jnp.transpose(item_ids, (1, 0, 2)), projected))
    return jnp.transpose(result, (1, 0, 2))
```

```python
import functools
import math

import jax
import jax.numpy as jnp
from jax import lax
from jax.experimental import pallas as pl
from jax.experimental.pallas import tpu as pltpu
from jax.sharding import PartitionSpec as P

MESH = pl.DeviceIdType.MESH
VMEM_SPEC = pl.BlockSpec(memory_space=pltpu.VMEM)
SMEM_SPEC = pl.BlockSpec(memory_space=pltpu.SMEM)
ANY_SPEC = pl.BlockSpec(memory_space=pl.ANY)
STEP = 16
LIMIT = 56 << 20


def greet(axis, n):
    me = lax.axis_index(axis)
    barrier = pltpu.get_barrier_semaphore()
    for d in range(1, n):
        pl.semaphore_signal(
            barrier, inc=1, device_id={axis: lax.rem(me + d, n)}, device_id_type=MESH
        )
    pl.semaphore_wait(barrier, n - 1)


def push(src, dst, send, recv, axis, peer):
    return pltpu.make_async_remote_copy(
        src_ref=src,
        dst_ref=dst,
        send_sem=send,
        recv_sem=recv,
        device_id={axis: peer},
        device_id_type=MESH,
    )


def ids_kernel(n, ids_ref, feats_ref, ids_out, feats_out, send, recv):
    me = lax.axis_index("cand")
    greet("cand", n)
    copies = []
    for d in range(1, n):
        peer = lax.rem(me + d, n)
        copies.append(
            push(ids_ref.at[peer], ids_out.at[me], send.at[0, d], recv.at[0, d], "cand", peer)
        )
        copies.append(
            push(feats_ref, feats_out.at[me], send.at[1, d], recv.at[1, d], "cand", peer)
        )
    for copy in copies:
        copy.start()
    ids_out[me] = ids_ref[me]
    feats_out[me] = feats_ref[...]
    for copy in copies:
        copy.wait()


def widen(src, dst, rows):
    size = math.gcd(rows, 256)

    def body(i, carry):
        at = pl.multiple_of(i * size, size)
        dst[pl.ds(at, size), :] = src[pl.ds(at, size), :].astype(jnp.float32)
        return carry

    lax.fori_loop(0, rows // size, body, 0)


def narrow(src, dst, rows):
    size = math.gcd(rows, 256)

    def body(i, carry):
        at = pl.multiple_of(i * size, size)
        dst[pl.ds(at, size), :] = src[pl.ds(at, size), :].astype(jnp.bfloat16)
        return carry

    lax.fori_loop(0, rows // size, body, 0)


def gather_kernel(tab_dev, rows_dev, cap, ids, tab_ref, out_ref, wide, found):
    slots = out_ref.shape[0]
    widen(tab_ref, wide, tab_dev * rows_dev)

    def body(i, carry):
        at = pl.multiple_of(i * STEP, STEP)

        @pl.when(ids[at] >= 0)
        def _():
            for j in range(STEP):
                row = jnp.maximum(ids[at + j], 0)
                found[pl.ds(at + j, 1), :] = wide[pl.ds(row, 1), :]

        return carry

    lax.fori_loop(0, slots // STEP, body, 0)
    narrow(found, out_ref, slots)


def rows_kernel(
    n,
    n_table,
    found,
    feats,
    tower_w,
    tower_b,
    proj_w,
    returned,
    partial,
    w_held,
    p_held,
    send,
    recv,
    load,
):
    me = lax.axis_index("cand")
    w_copy = pltpu.make_async_copy(tower_w, w_held, load.at[0])
    p_copy = pltpu.make_async_copy(proj_w, p_held, load.at[1])
    w_copy.start()
    p_copy.start()
    greet("cand", n)
    copies = []
    for d in range(1, n):
        peer = lax.rem(me + d, n)
        copies.append(
            push(found.at[peer], returned.at[me], send.at[d], recv.at[d], "cand", peer)
        )
    for copy in copies:
        copy.start()
    returned[me] = found[me]
    depth, width = w_held.shape
    chunk = math.gcd(depth, 512)
    w_copy.wait()

    def body(k, acc):
        at = pl.multiple_of(k * chunk, chunk)
        return acc + jnp.dot(
            feats[:, pl.ds(at, chunk)],
            w_held[pl.ds(at, chunk), :],
            preferred_element_type=jnp.float32,
        )

    acc = lax.fori_loop(
        0, depth // chunk, body, jnp.zeros((feats.shape[0], width), jnp.float32)
    )
    tower = jnp.maximum(acc + tower_b[...], 0.0).astype(jnp.bfloat16)
    p_copy.wait()
    part = jnp.dot(tower, p_held[...], preferred_element_type=jnp.float32)
    quarter = partial.shape[1]
    for q in range(n_table):
        partial[q] = part[q * quarter : (q + 1) * quarter, :]
    for copy in copies:
        copy.wait()


def restore_kernel(tab_dev, embed, where, ret_ref, out_ref, wide, fetched):
    rows = out_ref.shape[0]
    widen(ret_ref, wide, wide.shape[0])

    def body(i, carry):
        at = pl.multiple_of(i * STEP, STEP)
        for j in range(STEP):
            fetched[pl.ds(at + j, 1), :] = wide[pl.ds(where[at + j], 1), :]
        return carry

    lax.fori_loop(0, tab_dev * rows // STEP, body, 0)
    for t in range(tab_dev):
        narrow(
            fetched.at[pl.ds(t * rows, rows), :],
            out_ref.at[:, pl.ds(t * embed, embed)],
            rows,
        )


def table_kernel(n, rows_ref, part_ref, bias_ref, mine, parts, biases, send, recv):
    me = lax.axis_index("table")
    count, width = rows_ref.shape[1:]
    greet("table", n)
    copies = []
    for d in range(1, n):
        peer = lax.rem(me + d, n)
        spot = pl.ds(pl.multiple_of(me * width, width), width)
        copies.append(
            push(rows_ref.at[peer], mine.at[:, spot], send.at[0, d], recv.at[0, d], "table", peer)
        )
        copies.append(
            push(part_ref.at[peer], parts.at[me], send.at[1, d], recv.at[1, d], "table", peer)
        )
        copies.append(
            push(bias_ref, biases.at[me], send.at[2, d], recv.at[2, d], "table", peer)
        )
    for copy in copies:
        copy.start()
    mine[:, pl.ds(pl.multiple_of(me * width, width), width)] = rows_ref[me]
    parts[me] = part_ref[me]
    biases[me] = bias_ref[...]
    for copy in copies:
        copy.wait()


def mlp_kernel(
    n_table,
    cand_dev,
    mine,
    parts,
    cross_w,
    cross_b,
    first,
    bias,
    second,
    second_b,
    task_w,
    task_b,
    out,
    crossed,
    acc,
):
    k = pl.program_id(0)

    @pl.when(k == 0)
    def _():
        total = parts[0]
        for q in range(1, n_table):
            total = total + parts[q]
        proj = total.astype(jnp.bfloat16).astype(jnp.float32)
        for r in range(proj.shape[0]):
            span = slice(r * cand_dev, (r + 1) * cand_dev)
            base = (mine[span, :].astype(jnp.float32) + proj[r : r + 1, :]).astype(jnp.bfloat16)
            crossed[span, :] = base
        base = crossed[...]
        wide = base.astype(jnp.float32)
        product = jnp.dot(base, cross_w[...], preferred_element_type=jnp.float32)
        crossed[...] = (wide * (product + cross_b[...]) + wide).astype(jnp.bfloat16)

    hidden = jnp.maximum(
        jnp.dot(crossed[...], first[0], preferred_element_type=jnp.float32) + bias[0], 0.0
    ).astype(jnp.bfloat16)
    term = jnp.dot(hidden, second[0], preferred_element_type=jnp.float32)

    @pl.when(k == 0)
    def _():
        acc[...] = term

    @pl.when(k > 0)
    def _():
        acc[...] += term

    @pl.when(k == n_table - 1)
    def _():
        top = jnp.maximum(acc[...] + second_b[...], 0.0).astype(jnp.bfloat16)
        scores = lax.dot_general(
            task_w[...], top, (((0,), (1,)), ((), ())), preferred_element_type=jnp.float32
        )
        out[...] = scores + task_b[...]


def on_device(
    user_feats,
    tower_weight,
    tower_bias,
    user_proj,
    item_ids,
    tables,
    cross_weight,
    cross_bias,
    mlp_first,
    first_bias,
    mlp_second,
    second_bias,
    task_weight,
    task_bias,
):
    n_cand = lax.axis_size("cand")
    n_table = lax.axis_size("table")
    tab_dev, requests, cand_dev = item_ids.shape
    rows_dev = tables.shape[1]
    embed = tables.shape[2]
    req_dev, user_width = user_feats.shape
    capacity = 2 * req_dev * cand_dev
    first_all = lax.all_gather(mlp_first, "table", axis=0)
    second_all = lax.all_gather(mlp_second, "table", axis=0)

    row_total = requests * cand_dev
    block = math.gcd(row_total, 512)
    blocks = row_total // block
    flat_ids = item_ids.reshape(tab_dev, row_total)
    owner_dev = flat_ids // rows_dev
    local_row = flat_ids % rows_dev
    owner_hot = (
        owner_dev[:, :, None] == jnp.arange(n_cand, dtype=jnp.int32)[None, None, :]
    ).astype(jnp.bfloat16)
    blocked_hot = owner_hot.reshape(tab_dev, blocks, block, n_cand)
    lower = (jnp.arange(block)[:, None] >= jnp.arange(block)[None, :]).astype(jnp.bfloat16)
    within = jnp.einsum("ij,tbjo->tbio", lower, blocked_hot, preferred_element_type=jnp.float32)
    hot_wide = blocked_hot.astype(jnp.float32)
    block_totals = jnp.sum(hot_wide, axis=2)
    before = jnp.cumsum(block_totals, axis=1) - block_totals
    running = within + before[:, :, None, :]
    slot_pos = (
        (jnp.sum(running * hot_wide, axis=3) - 1.0).astype(jnp.int32).reshape(tab_dev, row_total)
    )
    flat_slot = owner_dev * capacity + slot_pos
    digits = jnp.stack(
        [local_row % 32, local_row // 32 % 32, local_row // 1024, jnp.ones_like(local_row)], axis=-1
    ).astype(jnp.bfloat16)
    slot_blocks = jnp.transpose(flat_slot.reshape(tab_dev, blocks, block), (1, 0, 2))
    digit_blocks = jnp.transpose(digits.reshape(tab_dev, blocks, block, 4), (1, 0, 2, 3))
    slot_all = jnp.arange(n_cand * capacity, dtype=jnp.int32)

    def place(total, inputs):
        slot_block, digit_block = inputs
        hit = (slot_block[:, :, None] == slot_all[None, None, :]).astype(jnp.bfloat16)
        return (
            total
            + jnp.einsum("tif,tid->tfd", hit, digit_block, preferred_element_type=jnp.float32),
            None,
        )

    placed, _ = lax.scan(
        place, jnp.zeros((tab_dev, n_cand * capacity, 4), jnp.float32), (slot_blocks, digit_blocks)
    )
    value = placed[:, :, 0] + 32.0 * placed[:, :, 1] + 1024.0 * placed[:, :, 2]
    base_row = jnp.arange(tab_dev, dtype=jnp.int32)[:, None] * rows_dev
    send_rows = jnp.where(placed[:, :, 3] > 0.5, value.astype(jnp.int32) + base_row, -1)
    send_rows = jnp.transpose(send_rows.reshape(tab_dev, n_cand, capacity), (1, 0, 2))

    wanted, feats = pl.pallas_call(
        functools.partial(ids_kernel, n_cand),
        out_shape=(
            jax.ShapeDtypeStruct((n_cand, tab_dev, capacity), jnp.int32),
            jax.ShapeDtypeStruct((n_cand, req_dev, user_width), user_feats.dtype),
        ),
        in_specs=[VMEM_SPEC] * 2,
        out_specs=(VMEM_SPEC,) * 2,
        scratch_shapes=[
            pltpu.SemaphoreType.DMA((2, n_cand)),
            pltpu.SemaphoreType.DMA((2, n_cand)),
        ],
        compiler_params=pltpu.CompilerParams(collective_id=0, has_side_effects=True),
        name="ids",
    )(send_rows, user_feats)

    slots = n_cand * tab_dev * capacity
    found = pl.pallas_call(
        functools.partial(gather_kernel, tab_dev, rows_dev, capacity),
        out_shape=jax.ShapeDtypeStruct((slots, embed), tables.dtype),
        in_specs=[SMEM_SPEC, VMEM_SPEC],
        out_specs=VMEM_SPEC,
        scratch_shapes=[
            pltpu.VMEM((tab_dev * rows_dev, embed), jnp.float32),
            pltpu.VMEM((slots, embed), jnp.float32),
        ],
        compiler_params=pltpu.CompilerParams(vmem_limit_bytes=LIMIT),
        name="gather",
    )(wanted.reshape(slots), tables.reshape(tab_dev * rows_dev, embed))

    returned, partial = pl.pallas_call(
        functools.partial(rows_kernel, n_cand, n_table),
        out_shape=(
            jax.ShapeDtypeStruct((n_cand, tab_dev * capacity, embed), tables.dtype),
            jax.ShapeDtypeStruct((n_table, requests // n_table, user_proj.shape[1]), jnp.float32),
        ),
        in_specs=[VMEM_SPEC, VMEM_SPEC, ANY_SPEC, VMEM_SPEC, ANY_SPEC],
        out_specs=(VMEM_SPEC,) * 2,
        scratch_shapes=[
            pltpu.VMEM(tower_weight.shape, tower_weight.dtype),
            pltpu.VMEM(user_proj.shape, user_proj.dtype),
            pltpu.SemaphoreType.DMA((n_cand,)),
            pltpu.SemaphoreType.DMA((n_cand,)),
            pltpu.SemaphoreType.DMA((2,)),
        ],
        compiler_params=pltpu.CompilerParams(
            collective_id=1, has_side_effects=True, vmem_limit_bytes=LIMIT
        ),
        name="rows",
    )(
        found.reshape(n_cand, tab_dev * capacity, embed),
        feats.reshape(requests, user_width),
        tower_weight,
        tower_bias[None, :],
        user_proj,
    )

    where = (
        owner_dev * (tab_dev * capacity)
        + jnp.arange(tab_dev, dtype=jnp.int32)[:, None] * capacity
        + slot_pos
    )
    fetched = pl.pallas_call(
        functools.partial(restore_kernel, tab_dev, embed),
        out_shape=jax.ShapeDtypeStruct((row_total, tab_dev * embed), tables.dtype),
        in_specs=[SMEM_SPEC, VMEM_SPEC],
        out_specs=VMEM_SPEC,
        scratch_shapes=[
            pltpu.VMEM((slots, embed), jnp.float32),
            pltpu.VMEM((tab_dev * row_total, embed), jnp.float32),
        ],
        compiler_params=pltpu.CompilerParams(vmem_limit_bytes=LIMIT),
        name="restore",
    )(where.reshape(tab_dev * row_total), returned.reshape(slots, embed))

    rows_mine = row_total // n_table
    width = n_table * tab_dev * embed
    mine, parts, biases = pl.pallas_call(
        functools.partial(table_kernel, n_table),
        out_shape=(
            jax.ShapeDtypeStruct((rows_mine, width), tables.dtype),
            jax.ShapeDtypeStruct(partial.shape, jnp.float32),
            jax.ShapeDtypeStruct((n_table, 1, first_bias.shape[0]), jnp.float32),
        ),
        in_specs=[VMEM_SPEC] * 3,
        out_specs=(VMEM_SPEC,) * 3,
        scratch_shapes=[
            pltpu.SemaphoreType.DMA((3, n_table)),
            pltpu.SemaphoreType.DMA((3, n_table)),
        ],
        compiler_params=pltpu.CompilerParams(
            collective_id=2, has_side_effects=True, vmem_limit_bytes=LIMIT
        ),
        name="quarters",
    )(fetched.reshape(n_table, rows_mine, tab_dev * embed), partial, first_bias[None, :])

    tasks = task_weight.shape[1]
    d_top = mlp_second.shape[1]
    whole = lambda a: pl.BlockSpec(a.shape, lambda k: (0,) * a.ndim)
    each = lambda a: pl.BlockSpec((1,) + a.shape[1:], lambda k: (k, 0, 0))
    cross_b, second_b, task_b = cross_bias[None, :], second_bias[None, :], task_bias[:, None]
    logits = pl.pallas_call(
        functools.partial(mlp_kernel, n_table, cand_dev),
        out_shape=jax.ShapeDtypeStruct((tasks, rows_mine), jnp.float32),
        grid=(n_table,),
        in_specs=[
            whole(mine),
            whole(parts),
            whole(cross_weight),
            whole(cross_b),
            each(first_all),
            each(biases),
            each(second_all),
            whole(second_b),
            whole(task_weight),
            whole(task_b),
        ],
        out_specs=pl.BlockSpec((tasks, rows_mine), lambda k: (0, 0)),
        scratch_shapes=[
            pltpu.VMEM((rows_mine, width), jnp.bfloat16),
            pltpu.VMEM((rows_mine, d_top), jnp.float32),
        ],
        compiler_params=pltpu.CompilerParams(vmem_limit_bytes=LIMIT),
        name="mlp",
    )(mine, parts, cross_weight, cross_b, first_all, biases, second_all, second_b, task_weight, task_b)
    return logits.reshape(tasks, requests // n_table, cand_dev)


def solution(mesh):
    placed = (
        P("cand", None),
        P(None, "table"),
        P("table"),
        P("table", None),
        P("table", None, "cand"),
        P("table", "cand", None),
        P(),
        P(),
        P(None, "table"),
        P("table"),
        P("table", None),
        P(),
        P(),
        P(),
    )
    return jax.shard_map(
        on_device, mesh=mesh, in_specs=placed, out_specs=P(None, "table", "cand"), check_vma=False
    )
```

```python
import functools
import math

import jax
import jax.numpy as jnp
from jax import lax
from jax.experimental import pallas as pl
from jax.experimental.pallas import tpu as pltpu
from jax.sharding import PartitionSpec as P

MESH = pl.DeviceIdType.MESH
VMEM_SPEC = pl.BlockSpec(memory_space=pltpu.VMEM)
SMEM_SPEC = pl.BlockSpec(memory_space=pltpu.SMEM)
ANY_SPEC = pl.BlockSpec(memory_space=pl.ANY)
STEP = 16
CORES = 2
LIMIT = 56 << 20


def greet(axis, n):
    me = lax.axis_index(axis)
    barrier = pltpu.get_barrier_semaphore()
    for d in range(1, n):
        pl.semaphore_signal(
            barrier, inc=1, device_id={axis: lax.rem(me + d, n)}, device_id_type=MESH
        )
    pl.semaphore_wait(barrier, n - 1)


def push(src, dst, send, recv, axis, peer):
    return pltpu.make_async_remote_copy(
        src_ref=src,
        dst_ref=dst,
        send_sem=send,
        recv_sem=recv,
        device_id={axis: peer},
        device_id_type=MESH,
    )


def ids_kernel(n, ids_ref, feats_ref, ids_out, feats_out, send, recv):
    me = lax.axis_index("cand")
    greet("cand", n)
    copies = []
    for d in range(1, n):
        peer = lax.rem(me + d, n)
        copies.append(
            push(ids_ref.at[peer], ids_out.at[me], send.at[0, d], recv.at[0, d], "cand", peer)
        )
        copies.append(
            push(feats_ref, feats_out.at[me], send.at[1, d], recv.at[1, d], "cand", peer)
        )
    for copy in copies:
        copy.start()
    ids_out[me] = ids_ref[me]
    feats_out[me] = feats_ref[...]
    for copy in copies:
        copy.wait()


def widen(src, dst, rows):
    size = math.gcd(rows, 256)

    def body(i, carry):
        at = pl.multiple_of(i * size, size)
        dst[pl.ds(at, size), :] = src[pl.ds(at, size), :].astype(jnp.float32)
        return carry

    lax.fori_loop(0, rows // size, body, 0)


def narrow(src, dst, rows):
    size = math.gcd(rows, 256)

    def body(i, carry):
        at = pl.multiple_of(i * size, size)
        dst[pl.ds(at, size), :] = src[pl.ds(at, size), :].astype(jnp.bfloat16)
        return carry

    lax.fori_loop(0, rows // size, body, 0)


def gather_kernel(tab_dev, rows_dev, cap, ids, tab_ref, out_ref, wide, found):
    slots = out_ref.shape[0]
    widen(tab_ref, wide, tab_dev * rows_dev)

    def body(i, carry):
        at = pl.multiple_of(i * STEP, STEP)

        @pl.when(ids[at] >= 0)
        def _():
            for j in range(STEP):
                row = jnp.maximum(ids[at + j], 0)
                found[pl.ds(at + j, 1), :] = wide[pl.ds(row, 1), :]

        return carry

    lax.fori_loop(0, slots // STEP, body, 0)
    narrow(found, out_ref, slots)


def rows_kernel(
    n,
    n_table,
    found,
    feats,
    tower_w,
    tower_b,
    proj_w,
    first,
    second,
    bias,
    returned,
    partial,
    first_o,
    second_o,
    bias_o,
    w_held,
    p_held,
    send,
    recv,
    w_send,
    w_recv,
    load,
):
    me = lax.axis_index("cand")
    place = lax.axis_index("table")
    mate = place + 1 - 2 * lax.rem(place, CORES)
    w_copy = pltpu.make_async_copy(tower_w, w_held, load.at[0])
    p_copy = pltpu.make_async_copy(proj_w, p_held, load.at[1])
    w_copy.start()
    p_copy.start()
    barrier = pltpu.get_barrier_semaphore()
    for d in range(1, n):
        pl.semaphore_signal(
            barrier, inc=1, device_id={"cand": lax.rem(me + d, n)}, device_id_type=MESH
        )
    pl.semaphore_signal(barrier, inc=1, device_id={"table": mate}, device_id_type=MESH)
    pl.semaphore_wait(barrier, n)
    copies = []
    for d in range(1, n):
        peer = lax.rem(me + d, n)
        copies.append(
            push(found.at[peer], returned.at[me], send.at[d], recv.at[d], "cand", peer)
        )
    for i, (src, dst) in enumerate(((first, first_o), (second, second_o), (bias, bias_o))):
        copies.append(push(src, dst, w_send.at[i], w_recv.at[i], "table", mate))
    for copy in copies:
        copy.start()
    returned[me] = found[me]
    depth, width = w_held.shape
    chunk = math.gcd(depth, 512)
    w_copy.wait()

    def body(k, acc):
        at = pl.multiple_of(k * chunk, chunk)
        return acc + jnp.dot(
            feats[:, pl.ds(at, chunk)],
            w_held[pl.ds(at, chunk), :],
            preferred_element_type=jnp.float32,
        )

    acc = lax.fori_loop(
        0, depth // chunk, body, jnp.zeros((feats.shape[0], width), jnp.float32)
    )
    tower = jnp.maximum(acc + tower_b[...], 0.0).astype(jnp.bfloat16)
    p_copy.wait()
    part = jnp.dot(tower, p_held[...], preferred_element_type=jnp.float32)
    quarter = partial.shape[2]
    for q in range(n_table):
        partial[q // CORES, q % CORES] = part[q * quarter : (q + 1) * quarter, :]
    for copy in copies:
        copy.wait()


def restore_kernel(tab_dev, embed, where, ret_ref, out_ref, wide, fetched):
    rows = out_ref.shape[0]
    widen(ret_ref, wide, wide.shape[0])

    def body(i, carry):
        at = pl.multiple_of(i * STEP, STEP)
        for j in range(STEP):
            fetched[pl.ds(at + j, 1), :] = wide[pl.ds(where[at + j], 1), :]
        return carry

    lax.fori_loop(0, tab_dev * rows // STEP, body, 0)
    for t in range(tab_dev):
        narrow(
            fetched.at[pl.ds(t * rows, rows), :],
            out_ref.at[:, pl.ds(t * embed, embed)],
            rows,
        )


def table_kernel(n, rows_ref, part_ref, mine, parts, send, recv):
    me = lax.axis_index("table")
    width = rows_ref.shape[3]
    spot = pl.ds(pl.multiple_of(me * width, width), width)
    greet("table", n)
    copies = []
    for d in range(1, n):
        peer = lax.rem(me + d, n)
        core = lax.rem(peer, CORES)
        copies.append(
            push(
                rows_ref.at[:, core],
                mine.at[:, :, spot],
                send.at[0, d],
                recv.at[0, d],
                "table",
                peer,
            )
        )
        copies.append(
            push(
                part_ref.at[:, core], parts.at[me], send.at[1, d], recv.at[1, d], "table", peer
            )
        )
    for copy in copies:
        copy.start()
    core = lax.rem(me, CORES)
    for y in range(n // CORES):
        mine[y, :, spot] = rows_ref[y, core]
        parts[me, y] = part_ref[y, core]
    for copy in copies:
        copy.wait()


def mlp_kernel(
    n_table,
    cand_dev,
    mine,
    parts,
    cross_w,
    cross_b,
    first,
    first_o,
    bias,
    bias_o,
    second,
    second_o,
    second_b,
    task_w,
    task_b,
    out,
    cross_v,
    first_v,
    second_v,
    base,
    crossed,
    acc,
    sent,
    got,
    load,
    send,
    recv,
):
    me = lax.axis_index("table")
    core = lax.rem(me, CORES)
    level = me // CORES
    levels = n_table // CORES
    loads = [pltpu.make_async_copy(cross_w, cross_v, load.at[0])]
    for i, (one, two) in enumerate(((first, second), (first_o, second_o))):
        loads.append(pltpu.make_async_copy(one, first_v.at[i], load.at[1 + 2 * i]))
        loads.append(pltpu.make_async_copy(two, second_v.at[i], load.at[2 + 2 * i]))
    for copy in loads:
        copy.start()
    barrier = pltpu.get_barrier_semaphore()
    for d in range(1, levels):
        other = lax.rem(level + d, levels) * CORES + core
        pl.semaphore_signal(barrier, inc=1, device_id={"table": other}, device_id_type=MESH)
    pl.semaphore_wait(barrier, levels - 1)
    rows, width = base.shape
    tile = math.gcd(width, 256)
    hidden_tile = math.gcd(first.shape[1], 256)
    biases = (bias, bias_o)
    copies = []
    for d in range(1, levels + 1):
        at_level = lax.rem(level + d, levels)
        total = parts[0, at_level]
        for q in range(1, n_table):
            total = total + parts[q, at_level]
        proj = total.astype(jnp.bfloat16).astype(jnp.float32)
        for r in range(proj.shape[0]):
            span = slice(r * cand_dev, (r + 1) * cand_dev)
            base[span, :] = (
                mine[at_level, span, :].astype(jnp.float32) + proj[r : r + 1, :]
            ).astype(jnp.bfloat16)
        if d == 1:
            loads[0].wait()

        def cross(j, carry):
            at = pl.ds(pl.multiple_of(j * tile, tile), tile)
            product = jnp.dot(base[...], cross_v[:, at], preferred_element_type=jnp.float32)
            wide = base[:, at].astype(jnp.float32)
            crossed[:, at] = (wide * (product + cross_b[:, at]) + wide).astype(jnp.bfloat16)
            return carry

        lax.fori_loop(0, width // tile, cross, 0)
        acc[...] = jnp.zeros_like(acc)
        for i in range(CORES):
            if d == 1:
                loads[1 + 2 * i].wait()
                loads[2 + 2 * i].wait()

            def layer(j, carry):
                at = pl.ds(pl.multiple_of(j * hidden_tile, hidden_tile), hidden_tile)
                hidden = jnp.dot(
                    crossed[...], first_v[i, :, at], preferred_element_type=jnp.float32
                )
                hidden = jnp.maximum(hidden + biases[i][:, at], 0.0).astype(jnp.bfloat16)
                acc[...] += jnp.dot(
                    hidden, second_v[i, at, :], preferred_element_type=jnp.float32
                )
                return carry

            lax.fori_loop(0, first.shape[1] // hidden_tile, layer, 0)
        if d < levels:
            sent[d - 1] = acc[...].astype(jnp.bfloat16)
            copies.append(
                push(
                    sent.at[d - 1],
                    got.at[d - 1],
                    send.at[d - 1],
                    recv.at[d - 1],
                    "table",
                    at_level * CORES + core,
                )
            )
            copies[-1].start()
    for copy in copies:
        copy.wait()
    total = acc[...] + second_b[...]
    for d in range(levels - 1):
        total = total + got[d].astype(jnp.float32)
    top = jnp.maximum(total, 0.0).astype(jnp.bfloat16)
    scores = lax.dot_general(
        task_w[...], top, (((0,), (1,)), ((), ())), preferred_element_type=jnp.float32
    )
    out[...] = scores + task_b[...]


def on_device(
    user_feats,
    tower_weight,
    tower_bias,
    user_proj,
    item_ids,
    tables,
    cross_weight,
    cross_bias,
    mlp_first,
    first_bias,
    mlp_second,
    second_bias,
    task_weight,
    task_bias,
):
    n_cand = lax.axis_size("cand")
    n_table = lax.axis_size("table")
    tab_dev, requests, cand_dev = item_ids.shape
    rows_dev = tables.shape[1]
    embed = tables.shape[2]
    req_dev, user_width = user_feats.shape
    capacity = 2 * req_dev * cand_dev
    row_total = requests * cand_dev
    block = math.gcd(row_total, 512)
    blocks = row_total // block
    flat_ids = item_ids.reshape(tab_dev, row_total)
    owner_dev = flat_ids // rows_dev
    local_row = flat_ids % rows_dev
    owner_hot = (
        owner_dev[:, :, None] == jnp.arange(n_cand, dtype=jnp.int32)[None, None, :]
    ).astype(jnp.bfloat16)
    blocked_hot = owner_hot.reshape(tab_dev, blocks, block, n_cand)
    lower = (jnp.arange(block)[:, None] >= jnp.arange(block)[None, :]).astype(jnp.bfloat16)
    within = jnp.einsum("ij,tbjo->tbio", lower, blocked_hot, preferred_element_type=jnp.float32)
    hot_wide = blocked_hot.astype(jnp.float32)
    block_totals = jnp.sum(hot_wide, axis=2)
    before = jnp.cumsum(block_totals, axis=1) - block_totals
    running = within + before[:, :, None, :]
    slot_pos = (
        (jnp.sum(running * hot_wide, axis=3) - 1.0).astype(jnp.int32).reshape(tab_dev, row_total)
    )
    flat_slot = owner_dev * capacity + slot_pos
    digits = jnp.stack(
        [local_row % 32, local_row // 32 % 32, local_row // 1024, jnp.ones_like(local_row)], axis=-1
    ).astype(jnp.bfloat16)
    slot_blocks = jnp.transpose(flat_slot.reshape(tab_dev, blocks, block), (1, 0, 2))
    digit_blocks = jnp.transpose(digits.reshape(tab_dev, blocks, block, 4), (1, 0, 2, 3))
    slot_all = jnp.arange(n_cand * capacity, dtype=jnp.int32)

    def place(total, inputs):
        slot_block, digit_block = inputs
        hit = (slot_block[:, :, None] == slot_all[None, None, :]).astype(jnp.bfloat16)
        return (
            total
            + jnp.einsum("tif,tid->tfd", hit, digit_block, preferred_element_type=jnp.float32),
            None,
        )

    placed, _ = lax.scan(
        place, jnp.zeros((tab_dev, n_cand * capacity, 4), jnp.float32), (slot_blocks, digit_blocks)
    )
    value = placed[:, :, 0] + 32.0 * placed[:, :, 1] + 1024.0 * placed[:, :, 2]
    base_row = jnp.arange(tab_dev, dtype=jnp.int32)[:, None] * rows_dev
    send_rows = jnp.where(placed[:, :, 3] > 0.5, value.astype(jnp.int32) + base_row, -1)
    send_rows = jnp.transpose(send_rows.reshape(tab_dev, n_cand, capacity), (1, 0, 2))

    wanted, feats = pl.pallas_call(
        functools.partial(ids_kernel, n_cand),
        out_shape=(
            jax.ShapeDtypeStruct((n_cand, tab_dev, capacity), jnp.int32),
            jax.ShapeDtypeStruct((n_cand, req_dev, user_width), user_feats.dtype),
        ),
        in_specs=[VMEM_SPEC] * 2,
        out_specs=(VMEM_SPEC,) * 2,
        scratch_shapes=[
            pltpu.SemaphoreType.DMA((2, n_cand)),
            pltpu.SemaphoreType.DMA((2, n_cand)),
        ],
        compiler_params=pltpu.CompilerParams(collective_id=0, has_side_effects=True),
        name="ids",
    )(send_rows, user_feats)

    slots = n_cand * tab_dev * capacity
    found = pl.pallas_call(
        functools.partial(gather_kernel, tab_dev, rows_dev, capacity),
        out_shape=jax.ShapeDtypeStruct((slots, embed), tables.dtype),
        in_specs=[SMEM_SPEC, VMEM_SPEC],
        out_specs=VMEM_SPEC,
        scratch_shapes=[
            pltpu.VMEM((tab_dev * rows_dev, embed), jnp.float32),
            pltpu.VMEM((slots, embed), jnp.float32),
        ],
        compiler_params=pltpu.CompilerParams(vmem_limit_bytes=LIMIT),
        name="gather",
    )(wanted.reshape(slots), tables.reshape(tab_dev * rows_dev, embed))

    levels = n_table // CORES
    bias_row = first_bias[None, :]
    returned, partial, first_o, second_o, bias_o = pl.pallas_call(
        functools.partial(rows_kernel, n_cand, n_table),
        out_shape=(
            jax.ShapeDtypeStruct((n_cand, tab_dev * capacity, embed), tables.dtype),
            jax.ShapeDtypeStruct(
                (levels, CORES, requests // n_table, user_proj.shape[1]), jnp.float32
            ),
            jax.ShapeDtypeStruct(mlp_first.shape, mlp_first.dtype),
            jax.ShapeDtypeStruct(mlp_second.shape, mlp_second.dtype),
            jax.ShapeDtypeStruct(bias_row.shape, bias_row.dtype),
        ),
        in_specs=[VMEM_SPEC, VMEM_SPEC, ANY_SPEC, VMEM_SPEC, ANY_SPEC, ANY_SPEC, ANY_SPEC, VMEM_SPEC],
        out_specs=(VMEM_SPEC, VMEM_SPEC, ANY_SPEC, ANY_SPEC, VMEM_SPEC),
        scratch_shapes=[
            pltpu.VMEM(tower_weight.shape, tower_weight.dtype),
            pltpu.VMEM(user_proj.shape, user_proj.dtype),
            pltpu.SemaphoreType.DMA((n_cand,)),
            pltpu.SemaphoreType.DMA((n_cand,)),
            pltpu.SemaphoreType.DMA((3,)),
            pltpu.SemaphoreType.DMA((3,)),
            pltpu.SemaphoreType.DMA((2,)),
        ],
        compiler_params=pltpu.CompilerParams(
            collective_id=1, has_side_effects=True, vmem_limit_bytes=LIMIT
        ),
        name="rows",
    )(
        found.reshape(n_cand, tab_dev * capacity, embed),
        feats.reshape(requests, user_width),
        tower_weight,
        tower_bias[None, :],
        user_proj,
        mlp_first,
        mlp_second,
        bias_row,
    )

    where = (
        owner_dev * (tab_dev * capacity)
        + jnp.arange(tab_dev, dtype=jnp.int32)[:, None] * capacity
        + slot_pos
    )
    fetched = pl.pallas_call(
        functools.partial(restore_kernel, tab_dev, embed),
        out_shape=jax.ShapeDtypeStruct((row_total, tab_dev * embed), tables.dtype),
        in_specs=[SMEM_SPEC, VMEM_SPEC],
        out_specs=VMEM_SPEC,
        scratch_shapes=[
            pltpu.VMEM((slots, embed), jnp.float32),
            pltpu.VMEM((tab_dev * row_total, embed), jnp.float32),
        ],
        compiler_params=pltpu.CompilerParams(vmem_limit_bytes=LIMIT),
        name="restore",
    )(where.reshape(tab_dev * row_total), returned.reshape(slots, embed))

    rows_mine = row_total // n_table
    width = n_table * tab_dev * embed
    mine, parts = pl.pallas_call(
        functools.partial(table_kernel, n_table),
        out_shape=(
            jax.ShapeDtypeStruct((levels, rows_mine, width), tables.dtype),
            jax.ShapeDtypeStruct((n_table, levels) + partial.shape[2:], jnp.float32),
        ),
        in_specs=[VMEM_SPEC] * 2,
        out_specs=(VMEM_SPEC,) * 2,
        scratch_shapes=[
            pltpu.SemaphoreType.DMA((2, n_table)),
            pltpu.SemaphoreType.DMA((2, n_table)),
        ],
        compiler_params=pltpu.CompilerParams(
            collective_id=2, has_side_effects=True, vmem_limit_bytes=LIMIT
        ),
        name="quarters",
    )(fetched.reshape(levels, CORES, rows_mine, tab_dev * embed), partial)

    tasks = task_weight.shape[1]
    d_top = mlp_second.shape[1]
    logits = pl.pallas_call(
        functools.partial(mlp_kernel, n_table, cand_dev),
        out_shape=jax.ShapeDtypeStruct((tasks, rows_mine), jnp.float32),
        in_specs=[
            VMEM_SPEC,
            VMEM_SPEC,
            ANY_SPEC,
            VMEM_SPEC,
            ANY_SPEC,
            ANY_SPEC,
            VMEM_SPEC,
            VMEM_SPEC,
            ANY_SPEC,
            ANY_SPEC,
            VMEM_SPEC,
            VMEM_SPEC,
            VMEM_SPEC,
        ],
        out_specs=VMEM_SPEC,
        scratch_shapes=[
            pltpu.VMEM(cross_weight.shape, cross_weight.dtype),
            pltpu.VMEM((CORES,) + mlp_first.shape, mlp_first.dtype),
            pltpu.VMEM((CORES,) + mlp_second.shape, mlp_second.dtype),
            pltpu.VMEM((rows_mine, width), jnp.bfloat16),
            pltpu.VMEM((rows_mine, width), jnp.bfloat16),
            pltpu.VMEM((rows_mine, d_top), jnp.float32),
            pltpu.VMEM((levels - 1, rows_mine, d_top), jnp.bfloat16),
            pltpu.VMEM((levels - 1, rows_mine, d_top), jnp.bfloat16),
            pltpu.SemaphoreType.DMA((1 + 2 * CORES,)),
            pltpu.SemaphoreType.DMA((levels - 1,)),
            pltpu.SemaphoreType.DMA((levels - 1,)),
        ],
        compiler_params=pltpu.CompilerParams(
            collective_id=3, has_side_effects=True, vmem_limit_bytes=LIMIT
        ),
        name="mlp",
    )(
        mine,
        parts,
        cross_weight,
        cross_bias[None, :],
        mlp_first,
        first_o,
        bias_row,
        bias_o,
        mlp_second,
        second_o,
        second_bias[None, :],
        task_weight,
        task_bias[:, None],
    )
    return logits.reshape(tasks, requests // n_table, cand_dev)


def solution(mesh):
    placed = (
        P("cand", None),
        P(None, "table"),
        P("table"),
        P("table", None),
        P("table", None, "cand"),
        P("table", "cand", None),
        P(),
        P(),
        P(None, "table"),
        P("table"),
        P("table", None),
        P(),
        P(),
        P(),
    )
    return jax.shard_map(
        on_device, mesh=mesh, in_specs=placed, out_specs=P(None, "table", "cand"), check_vma=False
    )
```

```python
import functools
import math

import jax
import jax.numpy as jnp
from jax import lax
from jax.experimental import pallas as pl
from jax.experimental.pallas import tpu as pltpu
from jax.sharding import PartitionSpec as P

MESH = pl.DeviceIdType.MESH
VMEM_SPEC = pl.BlockSpec(memory_space=pltpu.VMEM)
SMEM_SPEC = pl.BlockSpec(memory_space=pltpu.SMEM)
ANY_SPEC = pl.BlockSpec(memory_space=pl.ANY)
STEP = 16
CORES = 2
LIMIT = 56 << 20


def push(src, dst, send, recv, axis, peer):
    return pltpu.make_async_remote_copy(
        src_ref=src,
        dst_ref=dst,
        send_sem=send,
        recv_sem=recv,
        device_id={axis: peer},
        device_id_type=MESH,
    )


def widen(src, dst, rows):
    size = math.gcd(rows, 256)

    def body(i, carry):
        at = pl.multiple_of(i * size, size)
        dst[pl.ds(at, size), :] = src[pl.ds(at, size), :].astype(jnp.float32)
        return carry

    lax.fori_loop(0, rows // size, body, 0)


def narrow(src, dst, rows):
    size = math.gcd(rows, 256)

    def body(i, carry):
        at = pl.multiple_of(i * size, size)
        dst[pl.ds(at, size), :] = src[pl.ds(at, size), :].astype(jnp.bfloat16)
        return carry

    lax.fori_loop(0, rows // size, body, 0)


def front_kernel(
    n,
    n_table,
    ids,
    where,
    feats,
    tab,
    tower_w,
    tower_b,
    proj_w,
    first,
    second,
    bias,
    mine,
    parts,
    first_o,
    second_o,
    bias_o,
    ids_v,
    ids_s,
    feats_v,
    feats_f,
    tab_v,
    wide,
    found,
    packed,
    returned,
    ret_wide,
    fetched,
    rows_out,
    partial,
    w_held,
    p_held,
    load,
    id_send,
    id_recv,
    row_send,
    row_recv,
    w_send,
    w_recv,
    part_send,
    part_recv,
    q_send,
    q_recv,
):
    me = lax.axis_index("cand")
    place = lax.axis_index("table")
    core = lax.rem(place, CORES)
    level = place // CORES
    levels = n_table // CORES
    mate = place + 1 - 2 * core
    tab_copy = pltpu.make_async_copy(tab, tab_v, load.at[0])
    w_copy = pltpu.make_async_copy(tower_w, w_held, load.at[1])
    p_copy = pltpu.make_async_copy(proj_w, p_held, load.at[2])
    tab_copy.start()
    barrier = pltpu.get_barrier_semaphore()
    for d in range(1, n):
        pl.semaphore_signal(
            barrier, inc=1, device_id={"cand": lax.rem(me + d, n)}, device_id_type=MESH
        )
    for d in range(1, n_table):
        pl.semaphore_signal(
            barrier,
            inc=1,
            device_id={"table": lax.rem(place + d, n_table)},
            device_id_type=MESH,
        )
    pl.semaphore_wait(barrier, n + n_table - 2)

    def id_copy(d):
        peer = lax.rem(me + d, n)
        return push(ids.at[peer], ids_v.at[me], id_send.at[0, d], id_recv.at[0, d], "cand", peer)

    def feat_copy(d):
        peer = lax.rem(me + d, n)
        return push(feats, feats_v.at[me], id_send.at[1, d], id_recv.at[1, d], "cand", peer)

    def row_copy(d):
        peer = lax.rem(me + d, n)
        return push(packed.at[peer], returned.at[me], row_send.at[d], row_recv.at[d], "cand", peer)

    def each(low, high, act):
        def body(d, carry):
            act(d)
            return carry

        lax.fori_loop(low, high, body, 0)

    each(1, n, lambda d: id_copy(d).start())
    each(1, n, lambda d: feat_copy(d).start())
    swaps = [
        push(src, dst, w_send.at[i], w_recv.at[i], "table", mate)
        for i, (src, dst) in enumerate(((first, first_o), (second, second_o), (bias, bias_o)))
    ]
    for copy in swaps:
        copy.start()
    ids_v[me] = ids[me]
    feats_v[me] = feats[...]
    tab_copy.wait()
    w_copy.start()
    p_copy.start()
    widen(tab_v, wide, wide.shape[0])
    each(1, n, lambda d: id_copy(d).wait())
    to_scalar = pltpu.make_async_copy(ids_v, ids_s, load.at[3])
    to_scalar.start()
    to_scalar.wait()

    per = found.shape[0]
    lanes = ids_s.shape[2]

    def gather(d, out):
        peer = lax.rem(me + d, n)

        def body(i, carry):
            at = pl.multiple_of(i * STEP, STEP)
            line = i // (lanes // STEP)
            spot = lax.rem(i, lanes // STEP) * STEP
            for j in range(STEP):
                row = jnp.maximum(ids_s[peer, line, spot + j], 0)
                found[pl.ds(at + j, 1), :] = wide[pl.ds(row, 1), :]
            return carry

        lax.fori_loop(0, per // STEP, body, 0)
        narrow(found, out.at[peer], per)

    def serve(d):
        gather(d, packed)
        row_copy(d).start()

    each(1, n, serve)
    gather(0, returned)

    each(1, n, lambda d: feat_copy(d).wait())
    step = feats.shape[0]
    for c in range(n):
        feats_f[c * step : (c + 1) * step, :] = feats_v[c].astype(jnp.float32)
    depth, width = w_held.shape
    chunk = math.gcd(depth, 512)
    w_copy.wait()

    def body(k, acc):
        at = pl.multiple_of(k * chunk, chunk)
        return acc + jnp.dot(
            feats_f[:, pl.ds(at, chunk)].astype(jnp.bfloat16),
            w_held[pl.ds(at, chunk), :],
            preferred_element_type=jnp.float32,
        )

    acc = lax.fori_loop(
        0, depth // chunk, body, jnp.zeros((feats_f.shape[0], width), jnp.float32)
    )
    tower = jnp.maximum(acc + tower_b[...], 0.0).astype(jnp.bfloat16)
    p_copy.wait()
    part = jnp.dot(tower, p_held[...], preferred_element_type=jnp.float32)
    quarter = partial.shape[2]
    for q in range(n_table):
        partial[q // CORES, q % CORES] = part[q * quarter : (q + 1) * quarter, :]

    part_copies = []
    for d in range(1, n_table):
        peer = lax.rem(place + d, n_table)
        part_copies.append(
            push(
                partial.at[:, lax.rem(peer, CORES)],
                parts.at[place],
                part_send.at[d],
                part_recv.at[d],
                "table",
                peer,
            )
        )
    for copy in part_copies:
        copy.start()
    for y in range(levels):
        parts[place, y] = partial[y, core]

    def arrive(d):
        @pl.when(d > 0)
        def _():
            row_copy(d).wait()

        source = lax.rem(me - d + n, n)
        at = pl.multiple_of(source * per, per)
        widen(returned.at[source], ret_wide.at[pl.ds(at, per), :], per)

    each(0, n, arrive)

    count = rows_out.shape[2]
    embed = wide.shape[1]
    tab_dev = rows_out.shape[3] // embed
    share = tab_dev * embed
    lane = pl.ds(pl.multiple_of(place * share, share), share)
    rows = n_table * count
    quarter_copies = []
    for turn in range(CORES - 1, -1, -1):
        target = lax.rem(core + turn, CORES)
        for y in range(levels):
            begin = (y * CORES + target) * count

            for t in range(tab_dev):

                def restore(i, carry):
                    at = pl.multiple_of(i * STEP, STEP)
                    for j in range(STEP):
                        fetched[pl.ds(at + j, 1), :] = wide_row(t * rows + begin + at + j)
                    return carry

                def wide_row(i):
                    return ret_wide[pl.ds(where[i], 1), :]

                lax.fori_loop(0, count // STEP, restore, 0)
                narrow(
                    fetched, rows_out.at[y, target, :, pl.ds(t * embed, embed)], count
                )
            for up in range(levels - 1, -1, -1):
                if turn == 0 and up == 0:
                    mine[y, :, lane] = rows_out[y, target]
                    continue
                peer = lax.rem(level + up, levels) * CORES + target
                spot = turn * levels + up
                copy = push(
                    rows_out.at[y, target],
                    mine.at[y, :, lane],
                    q_send.at[spot, y],
                    q_recv.at[spot, y],
                    "table",
                    peer,
                )
                copy.start()
                quarter_copies.append(copy)
    for copy in quarter_copies + part_copies + swaps:
        copy.wait()


def mlp_kernel(
    n_table,
    cand_dev,
    mine,
    parts,
    cross_w,
    cross_b,
    first,
    first_o,
    bias,
    bias_o,
    second,
    second_o,
    second_b,
    task_w,
    task_b,
    out,
    cross_v,
    first_v,
    second_v,
    base,
    crossed,
    acc,
    sent,
    got,
    load,
    send,
    recv,
):
    me = lax.axis_index("table")
    core = lax.rem(me, CORES)
    level = me // CORES
    levels = n_table // CORES
    loads = [pltpu.make_async_copy(cross_w, cross_v, load.at[0])]
    for i, (one, two) in enumerate(((first, second), (first_o, second_o))):
        loads.append(pltpu.make_async_copy(one, first_v.at[i], load.at[1 + 2 * i]))
        loads.append(pltpu.make_async_copy(two, second_v.at[i], load.at[2 + 2 * i]))
    for copy in loads:
        copy.start()
    barrier = pltpu.get_barrier_semaphore()
    for d in range(1, levels):
        other = lax.rem(level + d, levels) * CORES + core
        pl.semaphore_signal(barrier, inc=1, device_id={"table": other}, device_id_type=MESH)
    pl.semaphore_wait(barrier, levels - 1)
    rows, width = base.shape
    tile = math.gcd(width, 256)
    hidden_tile = math.gcd(first.shape[1], 256)
    biases = (bias, bias_o)
    copies = []
    for d in range(1, levels + 1):
        at_level = lax.rem(level + d, levels)
        total = parts[0, at_level]
        for q in range(1, n_table):
            total = total + parts[q, at_level]
        proj = total.astype(jnp.bfloat16).astype(jnp.float32)
        for r in range(proj.shape[0]):
            span = slice(r * cand_dev, (r + 1) * cand_dev)
            base[span, :] = (
                mine[at_level, span, :].astype(jnp.float32) + proj[r : r + 1, :]
            ).astype(jnp.bfloat16)
        if d == 1:
            loads[0].wait()

        def cross(j, carry):
            at = pl.ds(pl.multiple_of(j * tile, tile), tile)
            product = jnp.dot(base[...], cross_v[:, at], preferred_element_type=jnp.float32)
            wide = base[:, at].astype(jnp.float32)
            crossed[:, at] = (wide * (product + cross_b[:, at]) + wide).astype(jnp.bfloat16)
            return carry

        lax.fori_loop(0, width // tile, cross, 0)
        acc[...] = jnp.zeros_like(acc)
        for i in range(CORES):
            if d == 1:
                loads[1 + 2 * i].wait()
                loads[2 + 2 * i].wait()

            def layer(j, carry):
                at = pl.ds(pl.multiple_of(j * hidden_tile, hidden_tile), hidden_tile)
                hidden = jnp.dot(
                    crossed[...], first_v[i, :, at], preferred_element_type=jnp.float32
                )
                hidden = jnp.maximum(hidden + biases[i][:, at], 0.0).astype(jnp.bfloat16)
                acc[...] += jnp.dot(
                    hidden, second_v[i, at, :], preferred_element_type=jnp.float32
                )
                return carry

            lax.fori_loop(0, first.shape[1] // hidden_tile, layer, 0)
        if d < levels:
            sent[d - 1] = acc[...].astype(jnp.bfloat16)
            copies.append(
                push(
                    sent.at[d - 1],
                    got.at[d - 1],
                    send.at[d - 1],
                    recv.at[d - 1],
                    "table",
                    at_level * CORES + core,
                )
            )
            copies[-1].start()
    for copy in copies:
        copy.wait()
    total = acc[...] + second_b[...]
    for d in range(levels - 1):
        total = total + got[d].astype(jnp.float32)
    top = jnp.maximum(total, 0.0).astype(jnp.bfloat16)
    scores = lax.dot_general(
        task_w[...], top, (((0,), (1,)), ((), ())), preferred_element_type=jnp.float32
    )
    out[...] = scores + task_b[...]


def on_device(
    user_feats,
    tower_weight,
    tower_bias,
    user_proj,
    item_ids,
    tables,
    cross_weight,
    cross_bias,
    mlp_first,
    first_bias,
    mlp_second,
    second_bias,
    task_weight,
    task_bias,
):
    n_cand = lax.axis_size("cand")
    n_table = lax.axis_size("table")
    tab_dev, requests, cand_dev = item_ids.shape
    rows_dev = tables.shape[1]
    embed = tables.shape[2]
    req_dev, user_width = user_feats.shape
    capacity = 2 * req_dev * cand_dev
    row_total = requests * cand_dev
    block = math.gcd(row_total, 512)
    blocks = row_total // block
    flat_ids = item_ids.reshape(tab_dev, row_total)
    owner_dev = flat_ids // rows_dev
    local_row = flat_ids % rows_dev
    owner_hot = (
        owner_dev[:, :, None] == jnp.arange(n_cand, dtype=jnp.int32)[None, None, :]
    ).astype(jnp.bfloat16)
    blocked_hot = owner_hot.reshape(tab_dev, blocks, block, n_cand)
    lower = (jnp.arange(block)[:, None] >= jnp.arange(block)[None, :]).astype(jnp.bfloat16)
    within = jnp.einsum("ij,tbjo->tbio", lower, blocked_hot, preferred_element_type=jnp.float32)
    hot_wide = blocked_hot.astype(jnp.float32)
    block_totals = jnp.sum(hot_wide, axis=2)
    before = jnp.cumsum(block_totals, axis=1) - block_totals
    running = within + before[:, :, None, :]
    slot_pos = (
        (jnp.sum(running * hot_wide, axis=3) - 1.0).astype(jnp.int32).reshape(tab_dev, row_total)
    )
    flat_slot = owner_dev * capacity + slot_pos
    digits = jnp.stack(
        [local_row % 32, local_row // 32 % 32, local_row // 1024, jnp.ones_like(local_row)], axis=-1
    ).astype(jnp.bfloat16)
    slot_blocks = jnp.transpose(flat_slot.reshape(tab_dev, blocks, block), (1, 0, 2))
    digit_blocks = jnp.transpose(digits.reshape(tab_dev, blocks, block, 4), (1, 0, 2, 3))
    slot_all = jnp.arange(n_cand * capacity, dtype=jnp.int32)

    def place(total, inputs):
        slot_block, digit_block = inputs
        hit = (slot_block[:, :, None] == slot_all[None, None, :]).astype(jnp.bfloat16)
        return (
            total
            + jnp.einsum("tif,tid->tfd", hit, digit_block, preferred_element_type=jnp.float32),
            None,
        )

    placed, _ = lax.scan(
        place, jnp.zeros((tab_dev, n_cand * capacity, 4), jnp.float32), (slot_blocks, digit_blocks)
    )
    value = placed[:, :, 0] + 32.0 * placed[:, :, 1] + 1024.0 * placed[:, :, 2]
    base_row = jnp.arange(tab_dev, dtype=jnp.int32)[:, None] * rows_dev
    send_rows = jnp.where(placed[:, :, 3] > 0.5, value.astype(jnp.int32) + base_row, -1)
    send_rows = jnp.transpose(send_rows.reshape(tab_dev, n_cand, capacity), (1, 0, 2))

    where = (
        owner_dev * (tab_dev * capacity)
        + jnp.arange(tab_dev, dtype=jnp.int32)[:, None] * capacity
        + slot_pos
    )
    slots = n_cand * tab_dev * capacity
    per = tab_dev * capacity
    lanes = math.gcd(per, 128)
    levels = n_table // CORES
    bias_row = first_bias[None, :]
    quarter = requests // n_table
    rows_mine = row_total // n_table
    width = n_table * tab_dev * embed
    parts_shape = (levels, quarter, user_proj.shape[1])
    vmem = pltpu.VMEM
    dma = pltpu.SemaphoreType.DMA
    mine, parts, first_o, second_o, bias_o = pl.pallas_call(
        functools.partial(front_kernel, n_cand, n_table),
        out_shape=(
            jax.ShapeDtypeStruct((levels, rows_mine, width), tables.dtype),
            jax.ShapeDtypeStruct((n_table,) + parts_shape, jnp.float32),
            jax.ShapeDtypeStruct(mlp_first.shape, mlp_first.dtype),
            jax.ShapeDtypeStruct(mlp_second.shape, mlp_second.dtype),
            jax.ShapeDtypeStruct(bias_row.shape, bias_row.dtype),
        ),
        in_specs=[
            VMEM_SPEC,
            SMEM_SPEC,
            VMEM_SPEC,
            ANY_SPEC,
            ANY_SPEC,
            VMEM_SPEC,
            ANY_SPEC,
            ANY_SPEC,
            ANY_SPEC,
            VMEM_SPEC,
        ],
        out_specs=(VMEM_SPEC, VMEM_SPEC, ANY_SPEC, ANY_SPEC, VMEM_SPEC),
        scratch_shapes=[
            vmem((n_cand, per // lanes, lanes), jnp.int32),
            pltpu.SMEM((n_cand, per // lanes, lanes), jnp.int32),
            vmem((n_cand, req_dev, user_width), user_feats.dtype),
            vmem((requests, user_width), jnp.float32),
            vmem((tab_dev * rows_dev, embed), tables.dtype),
            vmem((tab_dev * rows_dev, embed), jnp.float32),
            vmem((per, embed), jnp.float32),
            vmem((n_cand, per, embed), tables.dtype),
            vmem((n_cand, per, embed), tables.dtype),
            vmem((slots, embed), jnp.float32),
            vmem((rows_mine, embed), jnp.float32),
            vmem((levels, CORES, rows_mine, tab_dev * embed), tables.dtype),
            vmem((levels, CORES) + parts_shape[1:], jnp.float32),
            vmem(tower_weight.shape, tower_weight.dtype),
            vmem(user_proj.shape, user_proj.dtype),
            dma((4,)),
            dma((2, n_cand)),
            dma((2, n_cand)),
            dma((n_cand,)),
            dma((n_cand,)),
            dma((3,)),
            dma((3,)),
            dma((n_table,)),
            dma((n_table,)),
            dma((n_table, levels)),
            dma((n_table, levels)),
        ],
        compiler_params=pltpu.CompilerParams(
            collective_id=0, has_side_effects=True, vmem_limit_bytes=LIMIT
        ),
        name="front",
    )(
        send_rows.reshape(n_cand, per // lanes, lanes),
        where.reshape(tab_dev * row_total),
        user_feats,
        tables.reshape(tab_dev * rows_dev, embed),
        tower_weight,
        tower_bias[None, :],
        user_proj,
        mlp_first,
        mlp_second,
        bias_row,
    )

    tasks = task_weight.shape[1]
    d_top = mlp_second.shape[1]
    logits = pl.pallas_call(
        functools.partial(mlp_kernel, n_table, cand_dev),
        out_shape=jax.ShapeDtypeStruct((tasks, rows_mine), jnp.float32),
        in_specs=[
            VMEM_SPEC,
            VMEM_SPEC,
            ANY_SPEC,
            VMEM_SPEC,
            ANY_SPEC,
            ANY_SPEC,
            VMEM_SPEC,
            VMEM_SPEC,
            ANY_SPEC,
            ANY_SPEC,
            VMEM_SPEC,
            VMEM_SPEC,
            VMEM_SPEC,
        ],
        out_specs=VMEM_SPEC,
        scratch_shapes=[
            pltpu.VMEM(cross_weight.shape, cross_weight.dtype),
            pltpu.VMEM((CORES,) + mlp_first.shape, mlp_first.dtype),
            pltpu.VMEM((CORES,) + mlp_second.shape, mlp_second.dtype),
            pltpu.VMEM((rows_mine, width), jnp.bfloat16),
            pltpu.VMEM((rows_mine, width), jnp.bfloat16),
            pltpu.VMEM((rows_mine, d_top), jnp.float32),
            pltpu.VMEM((levels - 1, rows_mine, d_top), jnp.bfloat16),
            pltpu.VMEM((levels - 1, rows_mine, d_top), jnp.bfloat16),
            pltpu.SemaphoreType.DMA((1 + 2 * CORES,)),
            pltpu.SemaphoreType.DMA((levels - 1,)),
            pltpu.SemaphoreType.DMA((levels - 1,)),
        ],
        compiler_params=pltpu.CompilerParams(
            collective_id=1, has_side_effects=True, vmem_limit_bytes=LIMIT
        ),
        name="mlp",
    )(
        mine,
        parts,
        cross_weight,
        cross_bias[None, :],
        mlp_first,
        first_o,
        bias_row,
        bias_o,
        mlp_second,
        second_o,
        second_bias[None, :],
        task_weight,
        task_bias[:, None],
    )
    return logits.reshape(tasks, requests // n_table, cand_dev)


def solution(mesh):
    placed = (
        P("cand", None),
        P(None, "table"),
        P("table"),
        P("table", None),
        P("table", None, "cand"),
        P("table", "cand", None),
        P(),
        P(),
        P(None, "table"),
        P("table"),
        P("table", None),
        P(),
        P(),
        P(),
    )
    return jax.shard_map(
        on_device, mesh=mesh, in_specs=placed, out_specs=P(None, "table", "cand"), check_vma=False
    )
```

```python
import functools
import math

import jax
import jax.numpy as jnp
from jax import lax
from jax.experimental import pallas as pl
from jax.experimental.pallas import tpu as pltpu
from jax.sharding import PartitionSpec as P

MESH = pl.DeviceIdType.MESH
VMEM_SPEC = pl.BlockSpec(memory_space=pltpu.VMEM)
SMEM_SPEC = pl.BlockSpec(memory_space=pltpu.SMEM)
ANY_SPEC = pl.BlockSpec(memory_space=pl.ANY)
STEP = 16
CORES = 2
LIMIT = 62 << 20


def push(src, dst, send, recv, axis, peer):
    return pltpu.make_async_remote_copy(
        src_ref=src,
        dst_ref=dst,
        send_sem=send,
        recv_sem=recv,
        device_id={axis: peer},
        device_id_type=MESH,
    )


def widen(src, dst, rows):
    size = math.gcd(rows, 256)

    def body(i, carry):
        at = pl.multiple_of(i * size, size)
        dst[pl.ds(at, size), :] = src[pl.ds(at, size), :].astype(jnp.float32)
        return carry

    lax.fori_loop(0, rows // size, body, 0)


def narrow(src, dst, rows):
    size = math.gcd(rows, 256)

    def body(i, carry):
        at = pl.multiple_of(i * size, size)
        dst[pl.ds(at, size), :] = src[pl.ds(at, size), :].astype(jnp.bfloat16)
        return carry

    lax.fori_loop(0, rows // size, body, 0)


def front_kernel(
    n,
    n_table,
    cand_dev,
    ids,
    where,
    feats,
    tab,
    tower_w,
    tower_b,
    proj_w,
    first,
    second,
    bias,
    cross_w,
    cross_b,
    second_b,
    task_w,
    task_b,
    out,
    ids_v,
    ids_s,
    feats_v,
    feats_f,
    tab_v,
    wide,
    found,
    returned,
    fetched,
    rows_out,
    partial,
    w_held,
    p_held,
    mine,
    parts,
    cross_v,
    first_v,
    second_v,
    biases,
    base,
    crossed,
    acc,
    sent,
    got,
    load,
    id_send,
    id_recv,
    row_send,
    row_recv,
    w_send,
    w_recv,
    part_send,
    part_recv,
    q_send,
    q_recv,
    top_send,
    top_recv,
):
    me = lax.axis_index("cand")
    place = lax.axis_index("table")
    core = lax.rem(place, CORES)
    level = place // CORES
    levels = n_table // CORES
    mate = place + 1 - 2 * core
    tab_copy = pltpu.make_async_copy(tab, tab_v.at[pl.ds(0, tab.shape[0]), :], load.at[0])
    w_copy = pltpu.make_async_copy(tower_w, w_held, load.at[1])
    p_copy = pltpu.make_async_copy(proj_w, p_held, load.at[2])
    held = [
        pltpu.make_async_copy(src, dst, load.at[4 + i])
        for i, (src, dst) in enumerate(
            ((cross_w, cross_v), (first, first_v.at[0]), (second, second_v.at[0]))
        )
    ]
    per = found.shape[0]
    tab_copy.start()
    barrier = pltpu.get_barrier_semaphore()
    for d in range(1, n):
        pl.semaphore_signal(
            barrier, inc=1, device_id={"cand": lax.rem(me + d, n)}, device_id_type=MESH
        )
    for d in range(1, n_table):
        pl.semaphore_signal(
            barrier,
            inc=1,
            device_id={"table": lax.rem(place + d, n_table)},
            device_id_type=MESH,
        )
    pl.semaphore_wait(barrier, n + n_table - 2)

    def id_copy(d):
        peer = lax.rem(me + d, n)
        return push(ids.at[peer], ids_v.at[me], id_send.at[0, d], id_recv.at[0, d], "cand", peer)

    def feat_copy(d):
        peer = lax.rem(me + d, n)
        return push(feats, feats_v.at[me], id_send.at[1, d], id_recv.at[1, d], "cand", peer)

    def row_copy(d):
        peer = lax.rem(me + d, n)
        from_here = tab_v.at[pl.ds(pl.multiple_of(peer * per, per), per), :]
        return push(from_here, returned.at[me], row_send.at[d], row_recv.at[d], "cand", peer)

    def each(low, high, act):
        def body(d, carry):
            act(d)
            return carry

        lax.fori_loop(low, high, body, 0)

    each(1, n, lambda d: id_copy(d).start())
    each(1, n, lambda d: feat_copy(d).start())
    swaps = [
        push(src, dst, w_send.at[i], w_recv.at[i], "table", mate)
        for i, (src, dst) in enumerate(
            ((first, first_v.at[1]), (second, second_v.at[1]), (bias, biases.at[1]))
        )
    ]
    for copy in swaps:
        copy.start()
    biases[0] = bias[...]
    ids_v[me] = ids[me]
    feats_v[me] = feats[...]
    tab_copy.wait()
    w_copy.start()
    p_copy.start()
    for copy in held:
        copy.start()
    widen(tab_v, wide, tab.shape[0])
    each(1, n, lambda d: id_copy(d).wait())
    to_scalar = pltpu.make_async_copy(ids_v, ids_s, load.at[3])
    to_scalar.start()
    to_scalar.wait()

    lanes = ids_s.shape[2]

    def gather(peer, out):

        def body(i, carry):
            at = pl.multiple_of(i * STEP, STEP)
            line = i // (lanes // STEP)
            spot = lax.rem(i, lanes // STEP) * STEP
            for j in range(STEP):
                row = jnp.maximum(ids_s[peer, line, spot + j], 0)
                found[pl.ds(at + j, 1), :] = wide[pl.ds(row, 1), :]
            return carry

        lax.fori_loop(0, per // STEP, body, 0)
        narrow(found, out, per)

    def serve(d):
        peer = lax.rem(me + d, n)
        gather(peer, tab_v.at[pl.ds(pl.multiple_of(peer * per, per), per), :])
        row_copy(d).start()

    each(1, n, serve)
    gather(me, returned.at[me])

    each(1, n, lambda d: feat_copy(d).wait())
    step = feats.shape[0]
    for c in range(n):
        feats_f[c * step : (c + 1) * step, :] = feats_v[c].astype(jnp.float32)
    depth, width = w_held.shape
    chunk = math.gcd(depth, 512)
    w_copy.wait()

    def body(k, acc):
        at = pl.multiple_of(k * chunk, chunk)
        return acc + jnp.dot(
            feats_f[:, pl.ds(at, chunk)].astype(jnp.bfloat16),
            w_held[pl.ds(at, chunk), :],
            preferred_element_type=jnp.float32,
        )

    summed = lax.fori_loop(
        0, depth // chunk, body, jnp.zeros((feats_f.shape[0], width), jnp.float32)
    )
    tower = jnp.maximum(summed + tower_b[...], 0.0).astype(jnp.bfloat16)
    p_copy.wait()
    part = jnp.dot(tower, p_held[...], preferred_element_type=jnp.float32)
    quarter = partial.shape[2]
    for q in range(n_table):
        partial[q // CORES, q % CORES] = part[q * quarter : (q + 1) * quarter, :]

    part_copies = []
    for d in range(1, n_table):
        peer = lax.rem(place + d, n_table)
        part_copies.append(
            push(
                partial.at[:, lax.rem(peer, CORES)],
                parts.at[place],
                part_send.at[d],
                part_recv.at[d],
                "table",
                peer,
            )
        )
    for copy in part_copies:
        copy.start()
    for y in range(levels):
        parts[place, y] = partial[y, core]

    def arrive(d):
        @pl.when(d > 0)
        def _():
            row_copy(d).wait()

        source = lax.rem(me - d + n, n)
        at = pl.multiple_of(source * per, per)
        widen(returned.at[source], wide.at[pl.ds(at, per), :], per)

    each(0, n, arrive)

    count = rows_out.shape[2]
    embed = wide.shape[1]
    tab_dev = rows_out.shape[3] // embed
    share = tab_dev * embed
    lane = pl.ds(pl.multiple_of(place * share, share), share)
    rows = n_table * count
    quarter_copies = {}
    for lv in range(levels):
        y = lax.rem(level + lv, levels)
        for turn in range(CORES - 1, -1, -1):
            target = lax.rem(core + turn, CORES)
            begin = (y * CORES + target) * count

            for t in range(tab_dev):

                def restore(i, carry):
                    at = pl.multiple_of(i * STEP, STEP)
                    for j in range(STEP):
                        source = where[t * rows + begin + at + j]
                        fetched[pl.ds(at + j, 1), :] = wide[pl.ds(source, 1), :]
                    return carry

                lax.fori_loop(0, count // STEP, restore, 0)
                narrow(fetched, rows_out.at[y, target, :, pl.ds(t * embed, embed)], count)
            for up in range(levels - 1, -1, -1):
                if turn == 0 and up == 0:
                    mine[y, :, lane] = rows_out[y, target]
                    continue
                spot = turn * levels + up
                copy = push(
                    rows_out.at[y, target],
                    mine.at[y, :, lane],
                    q_send.at[spot, lv],
                    q_recv.at[spot, lv],
                    "table",
                    lax.rem(level + up, levels) * CORES + target,
                )
                copy.start()
                quarter_copies[turn, up, lv] = copy

    for copy in part_copies + swaps:
        copy.wait()
    for copy in held:
        copy.wait()
    rows, width = base.shape
    tile = math.gcd(width, 256)
    hidden_tile = math.gcd(first.shape[1], 256)
    top_copies = []
    for d in range(1, levels + 1):
        at_level = lax.rem(level + d, levels)
        for (turn, up, lv), copy in quarter_copies.items():
            if (d + up) % levels == lv:
                copy.wait_recv()
        total = parts[0, at_level]
        for q in range(1, n_table):
            total = total + parts[q, at_level]
        proj = total.astype(jnp.bfloat16).astype(jnp.float32)
        for r in range(proj.shape[0]):
            span = slice(r * cand_dev, (r + 1) * cand_dev)
            base[span, :] = (
                mine[at_level, span, :].astype(jnp.float32) + proj[r : r + 1, :]
            ).astype(jnp.bfloat16)

        def cross(j, carry):
            at = pl.ds(pl.multiple_of(j * tile, tile), tile)
            product = jnp.dot(base[...], cross_v[:, at], preferred_element_type=jnp.float32)
            broad = base[:, at].astype(jnp.float32)
            crossed[:, at] = (broad * (product + cross_b[:, at]) + broad).astype(jnp.bfloat16)
            return carry

        lax.fori_loop(0, width // tile, cross, 0)
        acc[...] = jnp.zeros_like(acc)
        for i in range(CORES):

            def layer(j, carry):
                at = pl.ds(pl.multiple_of(j * hidden_tile, hidden_tile), hidden_tile)
                hidden = jnp.dot(
                    crossed[...], first_v[i, :, at], preferred_element_type=jnp.float32
                )
                hidden = jnp.maximum(hidden + biases[i, :, at], 0.0).astype(jnp.bfloat16)
                acc[...] += jnp.dot(
                    hidden, second_v[i, at, :], preferred_element_type=jnp.float32
                )
                return carry

            lax.fori_loop(0, first.shape[1] // hidden_tile, layer, 0)
        if d < levels:
            sent[d - 1] = acc[...].astype(jnp.bfloat16)
            top_copies.append(
                push(
                    sent.at[d - 1],
                    got.at[d - 1],
                    top_send.at[d - 1],
                    top_recv.at[d - 1],
                    "table",
                    at_level * CORES + core,
                )
            )
            top_copies[-1].start()
    for copy in quarter_copies.values():
        copy.wait_send()
    for copy in top_copies:
        copy.wait()
    total = acc[...] + second_b[...]
    for d in range(levels - 1):
        total = total + got[d].astype(jnp.float32)
    top = jnp.maximum(total, 0.0).astype(jnp.bfloat16)
    scores = lax.dot_general(
        task_w[...], top, (((1,), (1,)), ((), ())), preferred_element_type=jnp.float32
    )
    for k in range(out.shape[0]):
        out[k : k + 1, :] = scores[k : k + 1, :] + task_b[k]


def on_device(
    user_feats,
    tower_weight,
    tower_bias,
    user_proj,
    item_ids,
    tables,
    cross_weight,
    cross_bias,
    mlp_first,
    first_bias,
    mlp_second,
    second_bias,
    task_weight,
    task_bias,
):
    n_cand = lax.axis_size("cand")
    n_table = lax.axis_size("table")
    tab_dev, requests, cand_dev = item_ids.shape
    rows_dev = tables.shape[1]
    embed = tables.shape[2]
    req_dev, user_width = user_feats.shape
    capacity = 2 * req_dev * cand_dev
    row_total = requests * cand_dev
    block = math.gcd(row_total, 512)
    blocks = row_total // block
    flat_ids = item_ids.reshape(tab_dev, row_total)
    owner_dev = flat_ids // rows_dev
    local_row = flat_ids % rows_dev
    owner_hot = (
        owner_dev[:, :, None] == jnp.arange(n_cand, dtype=jnp.int32)[None, None, :]
    ).astype(jnp.bfloat16)
    blocked_hot = owner_hot.reshape(tab_dev, blocks, block, n_cand)
    lower = (jnp.arange(block)[:, None] >= jnp.arange(block)[None, :]).astype(jnp.bfloat16)
    within = jnp.einsum("ij,tbjo->tbio", lower, blocked_hot, preferred_element_type=jnp.float32)
    hot_wide = blocked_hot.astype(jnp.float32)
    block_totals = jnp.sum(hot_wide, axis=2)
    before = jnp.cumsum(block_totals, axis=1) - block_totals
    running = within + before[:, :, None, :]
    slot_pos = (
        (jnp.sum(running * hot_wide, axis=3) - 1.0).astype(jnp.int32).reshape(tab_dev, row_total)
    )
    flat_slot = owner_dev * capacity + slot_pos
    digits = jnp.stack(
        [local_row % 32, local_row // 32 % 32, local_row // 1024, jnp.ones_like(local_row)], axis=-1
    ).astype(jnp.bfloat16)
    slot_blocks = jnp.transpose(flat_slot.reshape(tab_dev, blocks, block), (1, 0, 2))
    digit_blocks = jnp.transpose(digits.reshape(tab_dev, blocks, block, 4), (1, 0, 2, 3))
    slot_all = jnp.arange(n_cand * capacity, dtype=jnp.int32)

    def place(total, inputs):
        slot_block, digit_block = inputs
        hit = (slot_block[:, :, None] == slot_all[None, None, :]).astype(jnp.bfloat16)
        return (
            total
            + jnp.einsum("tif,tid->tfd", hit, digit_block, preferred_element_type=jnp.float32),
            None,
        )

    placed, _ = lax.scan(
        place, jnp.zeros((tab_dev, n_cand * capacity, 4), jnp.float32), (slot_blocks, digit_blocks)
    )
    value = placed[:, :, 0] + 32.0 * placed[:, :, 1] + 1024.0 * placed[:, :, 2]
    base_row = jnp.arange(tab_dev, dtype=jnp.int32)[:, None] * rows_dev
    send_rows = jnp.where(placed[:, :, 3] > 0.5, value.astype(jnp.int32) + base_row, -1)
    send_rows = jnp.transpose(send_rows.reshape(tab_dev, n_cand, capacity), (1, 0, 2))

    where = (
        owner_dev * (tab_dev * capacity)
        + jnp.arange(tab_dev, dtype=jnp.int32)[:, None] * capacity
        + slot_pos
    )
    slots = n_cand * tab_dev * capacity
    per = tab_dev * capacity
    lanes = math.gcd(per, 128)
    levels = n_table // CORES
    bias_row = first_bias[None, :]
    quarter = requests // n_table
    rows_mine = row_total // n_table
    width = n_table * tab_dev * embed
    parts_shape = (levels, quarter, user_proj.shape[1])
    vmem = pltpu.VMEM
    dma = pltpu.SemaphoreType.DMA
    tasks = task_weight.shape[1]
    d_top = mlp_second.shape[1]
    held_rows = max(tab_dev * rows_dev, slots)
    logits = pl.pallas_call(
        functools.partial(front_kernel, n_cand, n_table, cand_dev),
        out_shape=jax.ShapeDtypeStruct((tasks, rows_mine), jnp.float32),
        in_specs=[
            VMEM_SPEC,
            SMEM_SPEC,
            VMEM_SPEC,
            ANY_SPEC,
            ANY_SPEC,
            VMEM_SPEC,
            ANY_SPEC,
            ANY_SPEC,
            ANY_SPEC,
            VMEM_SPEC,
            ANY_SPEC,
            VMEM_SPEC,
            VMEM_SPEC,
            VMEM_SPEC,
            SMEM_SPEC,
        ],
        out_specs=VMEM_SPEC,
        scratch_shapes=[
            vmem((n_cand, per // lanes, lanes), jnp.int32),
            pltpu.SMEM((n_cand, per // lanes, lanes), jnp.int32),
            vmem((n_cand, req_dev, user_width), user_feats.dtype),
            vmem((requests, user_width), jnp.float32),
            vmem((held_rows, embed), tables.dtype),
            vmem((held_rows, embed), jnp.float32),
            vmem((per, embed), jnp.float32),
            vmem((n_cand, per, embed), tables.dtype),
            vmem((rows_mine, embed), jnp.float32),
            vmem((levels, CORES, rows_mine, tab_dev * embed), tables.dtype),
            vmem((levels, CORES) + parts_shape[1:], jnp.float32),
            vmem(tower_weight.shape, tower_weight.dtype),
            vmem(user_proj.shape, user_proj.dtype),
            vmem((levels, rows_mine, width), tables.dtype),
            vmem((n_table,) + parts_shape, jnp.float32),
            vmem(cross_weight.shape, cross_weight.dtype),
            vmem((CORES,) + mlp_first.shape, mlp_first.dtype),
            vmem((CORES,) + mlp_second.shape, mlp_second.dtype),
            vmem((CORES,) + bias_row.shape, bias_row.dtype),
            vmem((rows_mine, width), jnp.bfloat16),
            vmem((rows_mine, width), jnp.bfloat16),
            vmem((rows_mine, d_top), jnp.float32),
            vmem((levels - 1, rows_mine, d_top), jnp.bfloat16),
            vmem((levels - 1, rows_mine, d_top), jnp.bfloat16),
            dma((7,)),
            dma((2, n_cand)),
            dma((2, n_cand)),
            dma((n_cand,)),
            dma((n_cand,)),
            dma((3,)),
            dma((3,)),
            dma((n_table,)),
            dma((n_table,)),
            dma((n_table, levels)),
            dma((n_table, levels)),
            dma((levels - 1,)),
            dma((levels - 1,)),
        ],
        compiler_params=pltpu.CompilerParams(
            collective_id=0, has_side_effects=True, vmem_limit_bytes=LIMIT
        ),
        name="whole",
    )(
        send_rows.reshape(n_cand, per // lanes, lanes),
        where.reshape(tab_dev * row_total),
        user_feats,
        tables.reshape(tab_dev * rows_dev, embed),
        tower_weight,
        tower_bias[None, :],
        user_proj,
        mlp_first,
        mlp_second,
        bias_row,
        cross_weight,
        cross_bias[None, :],
        second_bias[None, :],
        task_weight.T,
        task_bias,
    )
    return logits.reshape(tasks, requests // n_table, cand_dev)


def solution(mesh):
    placed = (
        P("cand", None),
        P(None, "table"),
        P("table"),
        P("table", None),
        P("table", None, "cand"),
        P("table", "cand", None),
        P(),
        P(),
        P(None, "table"),
        P("table"),
        P("table", None),
        P(),
        P(),
        P(),
    )
    return jax.shard_map(
        on_device, mesh=mesh, in_specs=placed, out_specs=P(None, "table", "cand"), check_vma=False
    )
```

```python
import functools
import math

import jax
import jax.numpy as jnp
from jax import lax
from jax.experimental import pallas as pl
from jax.experimental.pallas import tpu as pltpu
from jax.sharding import PartitionSpec as P

MESH = pl.DeviceIdType.MESH
VMEM_SPEC = pl.BlockSpec(memory_space=pltpu.VMEM)
SMEM_SPEC = pl.BlockSpec(memory_space=pltpu.SMEM)
ANY_SPEC = pl.BlockSpec(memory_space=pl.ANY)
STEP = 16
CORES = 2
LIMIT = 62 << 20


def push(src, dst, send, recv, axis, peer):
    return pltpu.make_async_remote_copy(
        src_ref=src,
        dst_ref=dst,
        send_sem=send,
        recv_sem=recv,
        device_id={axis: peer},
        device_id_type=MESH,
    )


def widen(src, dst, rows):
    size = math.gcd(rows, 256)

    def body(i, carry):
        at = pl.multiple_of(i * size, size)
        dst[pl.ds(at, size), :] = src[pl.ds(at, size), :].astype(jnp.float32)
        return carry

    lax.fori_loop(0, rows // size, body, 0)


def narrow(src, dst, rows):
    size = math.gcd(rows, 256)

    def body(i, carry):
        at = pl.multiple_of(i * size, size)
        dst[pl.ds(at, size), :] = src[pl.ds(at, size), :].astype(jnp.bfloat16)
        return carry

    lax.fori_loop(0, rows // size, body, 0)


def front_kernel(
    n,
    n_table,
    cand_dev,
    ids,
    where,
    feats,
    tab,
    tower_w,
    tower_b,
    proj_w,
    first,
    second,
    bias,
    cross_w,
    cross_b,
    second_b,
    task_w,
    task_b,
    out,
    ids_v,
    ids_s,
    feats_v,
    feats_f,
    tab_v,
    wide,
    found,
    returned,
    fetched,
    rows_out,
    partial,
    w_held,
    p_held,
    mine,
    parts,
    cross_v,
    first_v,
    second_v,
    biases,
    base,
    crossed,
    acc,
    sent,
    got,
    load,
    id_send,
    id_recv,
    row_send,
    row_recv,
    w_send,
    w_recv,
    part_send,
    part_recv,
    q_send,
    q_recv,
    top_send,
    top_recv,
):
    me = lax.axis_index("cand")
    place = lax.axis_index("table")
    core = lax.rem(place, CORES)
    level = place // CORES
    levels = n_table // CORES
    mate = place + 1 - 2 * core
    tab_copy = pltpu.make_async_copy(tab, tab_v.at[pl.ds(0, tab.shape[0]), :], load.at[0])
    w_copy = pltpu.make_async_copy(tower_w, w_held, load.at[1])
    p_copy = pltpu.make_async_copy(proj_w, p_held, load.at[2])
    held = [
        pltpu.make_async_copy(src, dst, load.at[4 + i])
        for i, (src, dst) in enumerate(
            ((cross_w, cross_v), (first, first_v.at[0]), (second, second_v.at[0]))
        )
    ]
    per = found.shape[0]
    tab_copy.start()
    barrier = pltpu.get_barrier_semaphore()
    for d in range(1, n):
        pl.semaphore_signal(
            barrier, inc=1, device_id={"cand": lax.rem(me + d, n)}, device_id_type=MESH
        )
    for d in range(1, n_table):
        pl.semaphore_signal(
            barrier,
            inc=1,
            device_id={"table": lax.rem(place + d, n_table)},
            device_id_type=MESH,
        )
    pl.semaphore_wait(barrier, n + n_table - 2)

    def id_copy(d):
        peer = lax.rem(me + d, n)
        return push(ids.at[peer], ids_v.at[me], id_send.at[0, d], id_recv.at[0, d], "cand", peer)

    def feat_copy(d):
        peer = lax.rem(me + d, n)
        return push(feats, feats_v.at[me], id_send.at[1, d], id_recv.at[1, d], "cand", peer)

    def row_copy(d):
        peer = lax.rem(me + d, n)
        from_here = tab_v.at[pl.ds(pl.multiple_of(peer * per, per), per), :]
        return push(from_here, returned.at[me], row_send.at[d], row_recv.at[d], "cand", peer)

    def each(low, high, act):
        def body(d, carry):
            act(d)
            return carry

        lax.fori_loop(low, high, body, 0)

    each(1, n, lambda d: id_copy(d).start())
    each(1, n, lambda d: feat_copy(d).start())
    swaps = [
        push(src, dst, w_send.at[i], w_recv.at[i], "table", mate)
        for i, (src, dst) in enumerate(
            ((first, first_v.at[1]), (second, second_v.at[1]), (bias, biases.at[1]))
        )
    ]
    for copy in swaps:
        copy.start()
    biases[0] = bias[...]
    ids_v[me] = ids[me]
    feats_v[me] = feats[...]
    tab_copy.wait()
    w_copy.start()
    p_copy.start()
    for copy in held:
        copy.start()
    widen(tab_v, wide, tab.shape[0])
    each(1, n, lambda d: id_copy(d).wait())
    to_scalar = pltpu.make_async_copy(ids_v, ids_s, load.at[3])
    to_scalar.start()
    to_scalar.wait()

    lanes = ids_s.shape[2]

    def gather(peer, out):

        def body(i, carry):
            at = pl.multiple_of(i * STEP, STEP)
            line = i // (lanes // STEP)
            spot = lax.rem(i, lanes // STEP) * STEP
            for j in range(STEP):
                row = jnp.maximum(ids_s[peer, line, spot + j], 0)
                found[pl.ds(at + j, 1), :] = wide[pl.ds(row, 1), :]
            return carry

        lax.fori_loop(0, per // STEP, body, 0)
        narrow(found, out, per)

    def serve(d):
        peer = lax.rem(me + d, n)
        gather(peer, tab_v.at[pl.ds(pl.multiple_of(peer * per, per), per), :])
        row_copy(d).start()

    each(1, n, serve)
    gather(me, returned.at[me])

    each(1, n, lambda d: feat_copy(d).wait())
    step = feats.shape[0]
    for c in range(n):
        feats_f[c * step : (c + 1) * step, :] = feats_v[c].astype(jnp.float32)
    depth, width = w_held.shape
    chunk = math.gcd(depth, 512)
    w_copy.wait()

    def body(k, acc):
        at = pl.multiple_of(k * chunk, chunk)
        return acc + jnp.dot(
            feats_f[:, pl.ds(at, chunk)].astype(jnp.bfloat16),
            w_held[pl.ds(at, chunk), :],
            preferred_element_type=jnp.float32,
        )

    summed = lax.fori_loop(
        0, depth // chunk, body, jnp.zeros((feats_f.shape[0], width), jnp.float32)
    )
    tower = jnp.maximum(summed + tower_b[...], 0.0).astype(jnp.bfloat16)
    p_copy.wait()
    part = jnp.dot(tower, p_held[...], preferred_element_type=jnp.float32)
    quarter = partial.shape[2]
    for q in range(n_table):
        partial[q // CORES, q % CORES] = part[q * quarter : (q + 1) * quarter, :]

    part_copies = []
    for d in range(1, n_table):
        peer = lax.rem(place + d, n_table)
        part_copies.append(
            push(
                partial.at[:, lax.rem(peer, CORES)],
                parts.at[place],
                part_send.at[d],
                part_recv.at[d],
                "table",
                peer,
            )
        )
    for copy in part_copies:
        copy.start()
    for y in range(levels):
        parts[place, y] = partial[y, core]

    def arrive(d):
        @pl.when(d > 0)
        def _():
            row_copy(d).wait()

        source = lax.rem(me - d + n, n)
        at = pl.multiple_of(source * per, per)
        widen(returned.at[source], wide.at[pl.ds(at, per), :], per)

    each(0, n, arrive)

    count = rows_out.shape[2]
    embed = wide.shape[1]
    tab_dev = rows_out.shape[3] // embed
    share = tab_dev * embed
    lane = pl.ds(pl.multiple_of(place * share, share), share)
    rows = n_table * count
    quarter_copies = {}
    for lv in range(levels):
        y = lax.rem(level + lv, levels)
        for turn in range(CORES - 1, -1, -1):
            target = lax.rem(core + turn, CORES)
            begin = (y * CORES + target) * count

            for t in range(tab_dev):

                def restore(i, carry):
                    at = pl.multiple_of(i * STEP, STEP)
                    for j in range(STEP):
                        source = where[t * rows + begin + at + j]
                        fetched[pl.ds(at + j, 1), :] = wide[pl.ds(source, 1), :]
                    return carry

                lax.fori_loop(0, count // STEP, restore, 0)
                narrow(fetched, rows_out.at[y, target, :, pl.ds(t * embed, embed)], count)
            for up in range(levels - 1, -1, -1):
                if turn == 0 and up == 0:
                    mine[y, :, lane] = rows_out[y, target]
                    continue
                spot = turn * levels + up
                copy = push(
                    rows_out.at[y, target],
                    mine.at[y, :, lane],
                    q_send.at[spot, lv],
                    q_recv.at[spot, lv],
                    "table",
                    lax.rem(level + up, levels) * CORES + target,
                )
                copy.start()
                quarter_copies[turn, up, lv] = copy

    for copy in part_copies + swaps:
        copy.wait()
    for copy in held:
        copy.wait()
    rows, width = base.shape
    tile = math.gcd(width, 256)
    hidden_tile = math.gcd(first.shape[1], 256)
    units, d_top = second.shape
    top_tile = math.gcd(d_top, 256)
    top_copies = []
    for d in range(1, levels + 1):
        at_level = lax.rem(level + d, levels)
        for (turn, up, lv), copy in quarter_copies.items():
            if (d + up) % levels == lv:
                copy.wait_recv()
        total = parts[0, at_level]
        for q in range(1, n_table):
            total = total + parts[q, at_level]
        proj = total.astype(jnp.bfloat16).astype(jnp.float32)
        for r in range(proj.shape[0]):
            span = slice(r * cand_dev, (r + 1) * cand_dev)
            base[span, :] = (
                mine[at_level, span, :].astype(jnp.float32) + proj[r : r + 1, :]
            ).astype(jnp.bfloat16)

        def cross(j, carry):
            at = pl.ds(pl.multiple_of(j * tile, tile), tile)
            product = jnp.dot(base[...], cross_v[:, at], preferred_element_type=jnp.float32)
            broad = base[:, at].astype(jnp.float32)
            crossed[:, at] = (broad * (product + cross_b[:, at]) + broad).astype(jnp.bfloat16)
            return carry

        lax.fori_loop(0, width // tile, cross, 0)
        for i in range(CORES):

            def layer(j, carry):
                at = pl.ds(pl.multiple_of(j * hidden_tile, hidden_tile), hidden_tile)
                hidden = jnp.dot(
                    crossed[...], first_v[i, :, at], preferred_element_type=jnp.float32
                )
                hidden = jnp.maximum(hidden + biases[i, :, at], 0.0)
                w_held[i * rows : (i + 1) * rows, at] = hidden.astype(jnp.bfloat16)
                return carry

            lax.fori_loop(0, units // hidden_tile, layer, 0)
        for c in range(d_top // top_tile):
            at = slice(c * top_tile, (c + 1) * top_tile)
            term = jnp.dot(
                w_held[0:rows, 0:units], second_v[0, :, at], preferred_element_type=jnp.float32
            )
            for i in range(1, CORES):
                term += jnp.dot(
                    w_held[i * rows : (i + 1) * rows, 0:units],
                    second_v[i, :, at],
                    preferred_element_type=jnp.float32,
                )
            if d == levels:
                acc[:, at] = term
                continue
            sent[d - 1, :, at] = term.astype(jnp.bfloat16)
            top_copies.append(
                push(
                    sent.at[d - 1, :, at],
                    got.at[d - 1, :, at],
                    top_send.at[d - 1, c],
                    top_recv.at[d - 1, c],
                    "table",
                    at_level * CORES + core,
                )
            )
            top_copies[-1].start()
    for copy in quarter_copies.values():
        copy.wait_send()
    for copy in top_copies:
        copy.wait()
    total = acc[...] + second_b[...]
    for d in range(levels - 1):
        total = total + got[d].astype(jnp.float32)
    top = jnp.maximum(total, 0.0).astype(jnp.bfloat16)
    scores = lax.dot_general(
        task_w[...], top, (((1,), (1,)), ((), ())), preferred_element_type=jnp.float32
    )
    for k in range(out.shape[0]):
        out[k : k + 1, :] = scores[k : k + 1, :] + task_b[k]


def on_device(
    user_feats,
    tower_weight,
    tower_bias,
    user_proj,
    item_ids,
    tables,
    cross_weight,
    cross_bias,
    mlp_first,
    first_bias,
    mlp_second,
    second_bias,
    task_weight,
    task_bias,
):
    n_cand = lax.axis_size("cand")
    n_table = lax.axis_size("table")
    tab_dev, requests, cand_dev = item_ids.shape
    rows_dev = tables.shape[1]
    embed = tables.shape[2]
    req_dev, user_width = user_feats.shape
    capacity = 2 * req_dev * cand_dev
    row_total = requests * cand_dev
    block = math.gcd(row_total, 512)
    blocks = row_total // block
    flat_ids = item_ids.reshape(tab_dev, row_total)
    owner_dev = flat_ids // rows_dev
    local_row = flat_ids % rows_dev
    owner_hot = (
        owner_dev[:, :, None] == jnp.arange(n_cand, dtype=jnp.int32)[None, None, :]
    ).astype(jnp.bfloat16)
    blocked_hot = owner_hot.reshape(tab_dev, blocks, block, n_cand)
    lower = (jnp.arange(block)[:, None] >= jnp.arange(block)[None, :]).astype(jnp.bfloat16)
    within = jnp.einsum("ij,tbjo->tbio", lower, blocked_hot, preferred_element_type=jnp.float32)
    hot_wide = blocked_hot.astype(jnp.float32)
    block_totals = jnp.sum(hot_wide, axis=2)
    before = jnp.cumsum(block_totals, axis=1) - block_totals
    running = within + before[:, :, None, :]
    slot_pos = (
        (jnp.sum(running * hot_wide, axis=3) - 1.0).astype(jnp.int32).reshape(tab_dev, row_total)
    )
    flat_slot = owner_dev * capacity + slot_pos
    digits = jnp.stack(
        [local_row % 32, local_row // 32 % 32, local_row // 1024, jnp.ones_like(local_row)], axis=-1
    ).astype(jnp.bfloat16)
    slot_blocks = jnp.transpose(flat_slot.reshape(tab_dev, blocks, block), (1, 0, 2))
    digit_blocks = jnp.transpose(digits.reshape(tab_dev, blocks, block, 4), (1, 0, 2, 3))
    slot_all = jnp.arange(n_cand * capacity, dtype=jnp.int32)

    def place(total, inputs):
        slot_block, digit_block = inputs
        hit = (slot_block[:, :, None] == slot_all[None, None, :]).astype(jnp.bfloat16)
        return (
            total
            + jnp.einsum("tif,tid->tfd", hit, digit_block, preferred_element_type=jnp.float32),
            None,
        )

    placed, _ = lax.scan(
        place, jnp.zeros((tab_dev, n_cand * capacity, 4), jnp.float32), (slot_blocks, digit_blocks)
    )
    value = placed[:, :, 0] + 32.0 * placed[:, :, 1] + 1024.0 * placed[:, :, 2]
    base_row = jnp.arange(tab_dev, dtype=jnp.int32)[:, None] * rows_dev
    send_rows = jnp.where(placed[:, :, 3] > 0.5, value.astype(jnp.int32) + base_row, -1)
    send_rows = jnp.transpose(send_rows.reshape(tab_dev, n_cand, capacity), (1, 0, 2))

    where = (
        owner_dev * (tab_dev * capacity)
        + jnp.arange(tab_dev, dtype=jnp.int32)[:, None] * capacity
        + slot_pos
    )
    slots = n_cand * tab_dev * capacity
    per = tab_dev * capacity
    lanes = math.gcd(per, 128)
    levels = n_table // CORES
    bias_row = first_bias[None, :]
    quarter = requests // n_table
    rows_mine = row_total // n_table
    width = n_table * tab_dev * embed
    parts_shape = (levels, quarter, user_proj.shape[1])
    vmem = pltpu.VMEM
    dma = pltpu.SemaphoreType.DMA
    tasks = task_weight.shape[1]
    d_top = mlp_second.shape[1]
    held_rows = max(tab_dev * rows_dev, slots)
    logits = pl.pallas_call(
        functools.partial(front_kernel, n_cand, n_table, cand_dev),
        out_shape=jax.ShapeDtypeStruct((tasks, rows_mine), jnp.float32),
        in_specs=[
            VMEM_SPEC,
            SMEM_SPEC,
            VMEM_SPEC,
            ANY_SPEC,
            ANY_SPEC,
            VMEM_SPEC,
            ANY_SPEC,
            ANY_SPEC,
            ANY_SPEC,
            VMEM_SPEC,
            ANY_SPEC,
            VMEM_SPEC,
            VMEM_SPEC,
            VMEM_SPEC,
            SMEM_SPEC,
        ],
        out_specs=VMEM_SPEC,
        scratch_shapes=[
            vmem((n_cand, per // lanes, lanes), jnp.int32),
            pltpu.SMEM((n_cand, per // lanes, lanes), jnp.int32),
            vmem((n_cand, req_dev, user_width), user_feats.dtype),
            vmem((requests, user_width), jnp.float32),
            vmem((held_rows, embed), tables.dtype),
            vmem((held_rows, embed), jnp.float32),
            vmem((per, embed), jnp.float32),
            vmem((n_cand, per, embed), tables.dtype),
            vmem((rows_mine, embed), jnp.float32),
            vmem((levels, CORES, rows_mine, tab_dev * embed), tables.dtype),
            vmem((levels, CORES) + parts_shape[1:], jnp.float32),
            vmem(tower_weight.shape, tower_weight.dtype),
            vmem(user_proj.shape, user_proj.dtype),
            vmem((levels, rows_mine, width), tables.dtype),
            vmem((n_table,) + parts_shape, jnp.float32),
            vmem(cross_weight.shape, cross_weight.dtype),
            vmem((CORES,) + mlp_first.shape, mlp_first.dtype),
            vmem((CORES,) + mlp_second.shape, mlp_second.dtype),
            vmem((CORES,) + bias_row.shape, bias_row.dtype),
            vmem((rows_mine, width), jnp.bfloat16),
            vmem((rows_mine, width), jnp.bfloat16),
            vmem((rows_mine, d_top), jnp.float32),
            vmem((levels - 1, rows_mine, d_top), jnp.bfloat16),
            vmem((levels - 1, rows_mine, d_top), jnp.bfloat16),
            dma((7,)),
            dma((2, n_cand)),
            dma((2, n_cand)),
            dma((n_cand,)),
            dma((n_cand,)),
            dma((3,)),
            dma((3,)),
            dma((n_table,)),
            dma((n_table,)),
            dma((n_table, levels)),
            dma((n_table, levels)),
            dma((levels - 1, d_top // math.gcd(d_top, 256))),
            dma((levels - 1, d_top // math.gcd(d_top, 256))),
        ],
        compiler_params=pltpu.CompilerParams(
            collective_id=0, has_side_effects=True, vmem_limit_bytes=LIMIT
        ),
        name="whole",
    )(
        send_rows.reshape(n_cand, per // lanes, lanes),
        where.reshape(tab_dev * row_total),
        user_feats,
        tables.reshape(tab_dev * rows_dev, embed),
        tower_weight,
        tower_bias[None, :],
        user_proj,
        mlp_first,
        mlp_second,
        bias_row,
        cross_weight,
        cross_bias[None, :],
        second_bias[None, :],
        task_weight.T,
        task_bias,
    )
    return logits.reshape(tasks, requests // n_table, cand_dev)


def solution(mesh):
    placed = (
        P("cand", None),
        P(None, "table"),
        P("table"),
        P("table", None),
        P("table", None, "cand"),
        P("table", "cand", None),
        P(),
        P(),
        P(None, "table"),
        P("table"),
        P("table", None),
        P(),
        P(),
        P(),
    )
    return jax.shard_map(
        on_device, mesh=mesh, in_specs=placed, out_specs=P(None, "table", "cand"), check_vma=False
    )
```
